32 devices in a mesh: blk: 8 (over y, x, core), req: 4 (over z).
Axes of the slice: x: 2, y: 2, z: 4, core: 2. Of those that a mesh axis runs over, the one named last changes fastest.
Arguments:
- verified_queries: bfloat16 [4, 16, 5, 1024], P('req', 'blk'), may hold values from -96 to 96
- new_keys: bfloat16 [4, 16, 5, 256], P('req', 'blk'), may hold values from -6 to 6
- verified_value_rows: bfloat16 [4, 16, 5, 256], P('req', 'blk'), may hold values from -6 to 6
- prior_round_keys: bfloat16 [4, 16, 5, 256], P('req', 'blk'), may hold values from -6 to 6
- prior_round_values: bfloat16 [4, 16, 5, 256], P('req', 'blk'), may hold values from -6 to 6
- accepted: int32 [4, 16], P('req', 'blk'), may hold values from 0 to 5
- group_id: int32 [4, 16], P('req'), may hold values from 0 to 15
- cache_len: int32 [4, 16], P('req'), may hold values from 0 to 8192, as said below
- slot_owner: int32 [4, 64], P('req'), may hold values from 0 to 15, as said below
- piece_cache_keys: bfloat16 [4, 64, 256, 256], P('req', 'blk'), may hold values from -6 to 6
- piece_cache_values: bfloat16 [4, 64, 256, 256], P('req', 'blk'), may hold values from -6 to 6
- shared_prompt_keys: bfloat16 [16, 256, 256], P('req', 'blk'), may hold values from -6 to 6
- shared_prompt_values: bfloat16 [16, 256, 256], P('req', 'blk'), may hold values from -6 to 6
- prompt_mask: int32 [16, 8], P('req', 'blk'), may hold values 0 or 1
Outputs:
- attended: bfloat16 [4, 16, 5, 1024], P('req', 'blk')
The draws below stay inside these ranges and needn't reach their ends.
Inputs may be any that keep to these rules, and one draw needn't show every extreme that they name: `slot_owner`: A request's cache is the concatenation, in piece order, of the pieces that name it. In every batch one request owns exactly 32 pieces and no request owns more. `cache_len`: A request's length is at most 256 times the number of pieces it owns and more than 256 times one fewer; in every batch one request holds exactly 8192 rows.
All inputs are finite; a program needn't handle non-finite values. No bound on the sum of `prompt_mask` on one device may be relied on, other than what follows from the above.
Results may differ from the reference program's by a relative error of at most 0.003.
Values may be sent and summed in bfloat16 or wider, within the bound.
No kernel may reach another device: no remote copies, remote signals or barrier semaphores. Data moves between devices by JAX's collectives and lax.ppermute only.
A program may use at most 64 MiB of HBM per device.

```python
import jax
import jax.numpy as jnp
from jax import lax

QUERY_HEADS = 16
KEY_HEADS = 4
HEAD_SIZE = 64
VERIFIED_COUNT = 5
PIECE_ROWS = 256
MOSTP = 32
BLOCK_ROWS = 32
BATCH_COUNT = 4
BATCH_REQUESTS = 16
PIECE_COUNT = 64
PROMPT_BLOCKS = 8
PROMPT_ROWS = 256
PROMPT_COUNT = 16


def piece_owner_draw(key):
    base_key = jax.random.fold_in(key, 11)

    def one_batch(row_key):
        first_part, second, third, fourth = jax.random.split(row_key, 4)
        longest = jax.random.randint(first_part, (), 0, BATCH_REQUESTS)
        order = jax.random.permutation(second, PIECE_COUNT)
        others = (longest + 1 + jnp.arange((BATCH_REQUESTS - 1) * MOSTP, dtype=jnp.int32) // MOSTP) % BATCH_REQUESTS
        others = jax.random.permutation(third, others)[:PIECE_COUNT - MOSTP]
        assigned = jnp.concatenate([jnp.full((MOSTP,), longest, jnp.int32), others.astype(jnp.int32)])
        owners = jnp.zeros((PIECE_COUNT,), jnp.int32).at[order].set(assigned)
        counts = jnp.sum((owners[:, None] == jnp.arange(BATCH_REQUESTS, dtype=jnp.int32)[None, :]).astype(jnp.int32), axis=0)
        extra = jax.random.randint(fourth, (BATCH_REQUESTS,), 1, PIECE_ROWS + 1)
        lengths = jnp.where(counts > 0, (counts - 1) * PIECE_ROWS + extra, 0)
        lengths = jnp.where(jnp.arange(BATCH_REQUESTS, dtype=jnp.int32) == longest, MOSTP * PIECE_ROWS, lengths)
        return (owners, lengths.astype(jnp.int32))
    return jax.vmap(one_batch)(jax.random.split(base_key, BATCH_COUNT))


def draw_slot_owner(key, part):
    return piece_owner_draw(key)[0]


def draw_cache_len(key, part):
    return piece_owner_draw(key)[1]


def drawn_rows(key):
    base_key = jax.random.fold_in(key, 23)
    first_part, second = jax.random.split(base_key, 2)
    verified_part = jnp.clip(jax.random.normal(first_part, (BATCH_COUNT, BATCH_REQUESTS, VERIFIED_COUNT, KEY_HEADS * HEAD_SIZE), jnp.float32), -6.0, 6.0)
    query_rows = jnp.clip(2.0 * jax.random.normal(second, (BATCH_COUNT, BATCH_REQUESTS, VERIFIED_COUNT, QUERY_HEADS * HEAD_SIZE), jnp.float32), -12.0, 12.0)
    return (query_rows, verified_part)


def draw_verified_queries(key, part):
    return drawn_rows(key)[0].astype(jnp.bfloat16)


def draw_new_keys(key, part):
    return drawn_rows(key)[1].astype(jnp.bfloat16)


def plant(result, stream_key, least, high):
    longest = result.shape.index(max(result.shape))
    spots = []
    for shift in (0, 1):
        where = [jax.random.randint(jax.random.fold_in(stream_key, axis), (), 0, length) for axis, length in enumerate(result.shape)]
        where[longest] = (where[longest] + shift) % result.shape[longest]
        spots.append(tuple(where))
    return result.at[spots[0]].set(least).at[spots[1]].set(high)


def block_scale(key, extent, cuts, low, top_value):
    factor_of, own = 1.0, jax.random.fold_in(key, 6)
    for dim, blocks in cuts:
        steps = jnp.exp(jax.random.uniform(jax.random.fold_in(own, dim), (blocks,), jnp.float32, low / len(cuts), top_value / len(cuts)))
        factor_of = factor_of * jnp.repeat(steps, extent[dim] // blocks).reshape([-1 if axis == dim else 1 for axis in range(len(extent))])
    return factor_of


def noise(key, extent, scale, reach, cuts=(), kind=jnp.bfloat16):
    drawn = jax.random.normal(key, extent, jnp.float32) * scale
    if len(cuts) > 0:
        drawn = block_scale(key, extent, cuts, -0.22, 0.18) * drawn
    return jnp.clip(drawn, min=-reach, max=reach).astype(kind)


def setup_inputs(seed: int = 0) -> dict:
    key_list = jax.random.split(jax.random.key(seed), 15)
    verified_queries = draw_verified_queries(jax.random.fold_in(key_list[14], 71), 0)
    new_keys = draw_new_keys(jax.random.fold_in(key_list[14], 71), 0)
    verified_value_rows = noise(key_list[2], (BATCH_COUNT, BATCH_REQUESTS, VERIFIED_COUNT, KEY_HEADS * HEAD_SIZE), 1.0, 6.0, ((0, 4), (1, 8)))
    prior_round_keys = noise(key_list[3], (BATCH_COUNT, BATCH_REQUESTS, VERIFIED_COUNT, KEY_HEADS * HEAD_SIZE), 1.0, 6.0, ((0, 4), (1, 8)))
    prior_round_values = noise(key_list[4], (BATCH_COUNT, BATCH_REQUESTS, VERIFIED_COUNT, KEY_HEADS * HEAD_SIZE), 1.0, 6.0, ((0, 4), (1, 8)))
    accepted = plant(jax.random.randint(key_list[5], (BATCH_COUNT, BATCH_REQUESTS), 0, VERIFIED_COUNT + 1), jax.random.fold_in(key_list[5], 1), 0, VERIFIED_COUNT).astype(jnp.int32)
    group_id = plant(jax.random.randint(key_list[6], (BATCH_COUNT, BATCH_REQUESTS), 0, PROMPT_COUNT), jax.random.fold_in(key_list[6], 1), 0, PROMPT_COUNT - 1).astype(jnp.int32)
    cache_len = draw_cache_len(jax.random.fold_in(key_list[14], 71), 0)
    slot_owner = draw_slot_owner(jax.random.fold_in(key_list[14], 71), 0)
    piece_cache_keys = noise(key_list[9], (BATCH_COUNT, PIECE_COUNT, PIECE_ROWS, KEY_HEADS * HEAD_SIZE), 1.0, 6.0, ((0, 4), (1, 8)))
    piece_cache_values = noise(key_list[10], (BATCH_COUNT, PIECE_COUNT, PIECE_ROWS, KEY_HEADS * HEAD_SIZE), 1.0, 6.0, ((0, 4), (1, 8)))
    shared_prompt_keys = noise(key_list[11], (PROMPT_COUNT, PROMPT_ROWS, KEY_HEADS * HEAD_SIZE), 1.0, 6.0, ((0, 4), (1, 8)))
    shared_prompt_values = noise(key_list[12], (PROMPT_COUNT, PROMPT_ROWS, KEY_HEADS * HEAD_SIZE), 1.0, 6.0, ((0, 4), (1, 8)))
    prompt_mask = plant((jax.random.randint(key_list[13], (PROMPT_COUNT, PROMPT_BLOCKS), 0, 4) < 3).astype(jnp.int32), jax.random.fold_in(key_list[13], 1), 0, 1)
    return dict(verified_queries=verified_queries, new_keys=new_keys, verified_value_rows=verified_value_rows, prior_round_keys=prior_round_keys, prior_round_values=prior_round_values, accepted=accepted, group_id=group_id, cache_len=cache_len, slot_owner=slot_owner, piece_cache_keys=piece_cache_keys, piece_cache_values=piece_cache_values, shared_prompt_keys=shared_prompt_keys, shared_prompt_values=shared_prompt_values, prompt_mask=prompt_mask)


LOWEST = -1e30


def block_weights(scores, live_rows):
    masked = jnp.where(live_rows, scores, LOWEST)
    ceiling = jnp.max(masked, axis=-1)
    weights = jnp.where(live_rows, jnp.exp(masked - ceiling[..., None]), 0.0).astype(jnp.bfloat16)
    return ceiling, weights, jnp.sum(weights.astype(jnp.float32), axis=-1)


def reference(verified_queries, new_keys, verified_value_rows, prior_round_keys, prior_round_values, accepted, group_id, cache_len, slot_owner, piece_cache_keys, piece_cache_values, shared_prompt_keys, shared_prompt_values, prompt_mask):
    heads_per_key = QUERY_HEADS // KEY_HEADS
    score_scale = HEAD_SIZE ** -0.5
    highest = lax.Precision.HIGHEST

    def one_batch(items):
        query_rows, verified_keys, verified_values, earlier_keys, earlier_values, taken, prompt_groups, lengths, owners, keys_of_piece, values_of_piece = items
        head_count = query_rows.reshape(BATCH_REQUESTS, VERIFIED_COUNT, KEY_HEADS, heads_per_key, HEAD_SIZE).astype(jnp.float32)
        request_keys = jnp.concatenate([earlier_keys, verified_keys], axis=1).reshape(BATCH_REQUESTS, 2 * VERIFIED_COUNT, KEY_HEADS, HEAD_SIZE).astype(jnp.float32)
        request_values = jnp.concatenate([earlier_values, verified_values], axis=1).reshape(BATCH_REQUESTS, 2 * VERIFIED_COUNT, KEY_HEADS, HEAD_SIZE).astype(jnp.float32)
        scores = jnp.einsum('rnkgd,rjkd->rkgnj', head_count, request_keys, precision=highest) * score_scale
        column = jnp.arange(2 * VERIFIED_COUNT, dtype=jnp.int32)
        position = jnp.arange(VERIFIED_COUNT, dtype=jnp.int32)
        live_prev = (column[None, :] < VERIFIED_COUNT) & (column[None, :] < taken[:, None])
        live_new = (column[None, :] >= VERIFIED_COUNT) & (column[None, :] - VERIFIED_COUNT <= position[:, None])
        live_rows = live_prev[:, None, None, None, :] | live_new[None, None, None, :, :]
        own_top, own_weights, own_mass = block_weights(scores, live_rows)
        own_part = jnp.einsum('rkgnj,rjkd->rkgnd', own_weights.astype(jnp.float32), request_values, precision=highest)

        keys_of_block = shared_prompt_keys[prompt_groups].reshape(BATCH_REQUESTS, PROMPT_BLOCKS, BLOCK_ROWS, KEY_HEADS, HEAD_SIZE).astype(jnp.float32)
        values_of_block = shared_prompt_values[prompt_groups].reshape(BATCH_REQUESTS, PROMPT_BLOCKS, BLOCK_ROWS, KEY_HEADS, HEAD_SIZE).astype(jnp.float32)
        block_live = prompt_mask[prompt_groups] == 1
        scores = jnp.einsum('rnkgd,rbjkd->rkgnbj', head_count, keys_of_block, precision=highest) * score_scale
        live_rows = jnp.broadcast_to(block_live[:, None, None, None, :, None], scores.shape)
        prompt_top, prompt_weights, prompt_mass = block_weights(scores, live_rows)
        prompt_part = jnp.einsum('rkgnbj,rbjkd->rkgnbd', prompt_weights.astype(jnp.float32), values_of_block, precision=highest)

        owner_table = (owners[:, None] == jnp.arange(BATCH_REQUESTS, dtype=jnp.int32)[None, :]).astype(jnp.int32)
        before = jnp.cumsum(owner_table, axis=0) - owner_table
        ranking = jnp.sum(before * owner_table, axis=1)
        filling = jnp.clip(lengths[owners] - ranking * PIECE_ROWS, 0, PIECE_ROWS)
        slot_query = head_count[owners]
        keys_of_slot = keys_of_piece.reshape(PIECE_COUNT, PIECE_ROWS, KEY_HEADS, HEAD_SIZE).astype(jnp.float32)
        values_of_slot = values_of_piece.reshape(PIECE_COUNT, PIECE_ROWS, KEY_HEADS, HEAD_SIZE).astype(jnp.float32)
        scores = jnp.einsum('snkgd,sjkd->skgnj', slot_query, keys_of_slot, precision=highest) * score_scale
        live_piece = jnp.arange(PIECE_ROWS, dtype=jnp.int32)[None, :] < filling[:, None]
        live_rows = jnp.broadcast_to(live_piece[:, None, None, None, :], scores.shape)
        slot_top, slot_weights, slot_mass = block_weights(scores, live_rows)
        slot_part = jnp.einsum('skgnj,sjkd->skgnd', slot_weights.astype(jnp.float32), values_of_slot, precision=highest)
        chosen = owner_table > 0
        slot_best = jnp.max(jnp.where(chosen[:, :, None, None, None], slot_top[:, None], LOWEST), axis=0)

        best_top = jnp.maximum(jnp.maximum(own_top, jnp.max(prompt_top, axis=-1)), slot_best)
        own_lift = jnp.exp(own_top - best_top)
        prompt_lift = jnp.exp(prompt_top - best_top[..., None])
        slot_lift = jnp.exp(slot_top - best_top[owners])
        overall_mass = own_lift * own_mass + jnp.sum(prompt_lift * prompt_mass, axis=-1) + jax.ops.segment_sum(slot_lift * slot_mass, owners, num_segments=BATCH_REQUESTS)
        overall_part = own_lift[..., None] * own_part + jnp.sum(prompt_lift[..., None] * prompt_part, axis=-2) + jax.ops.segment_sum(slot_lift[..., None] * slot_part, owners, num_segments=BATCH_REQUESTS)
        attention_output = overall_part / overall_mass[..., None]
        return attention_output.transpose(0, 3, 1, 2, 4).reshape(BATCH_REQUESTS, VERIFIED_COUNT, QUERY_HEADS * HEAD_SIZE).astype(jnp.bfloat16)

    return lax.map(one_batch, (verified_queries, new_keys, verified_value_rows, prior_round_keys, prior_round_values, accepted, group_id, cache_len, slot_owner, piece_cache_keys, piece_cache_values))
```

```python
import functools

import jax
import jax.numpy as jnp
from jax import lax
from jax.experimental import pallas as pl
from jax.experimental.pallas import tpu as pltpu
from jax.sharding import PartitionSpec as P

QUERY_HEADS = 16
KEY_HEADS = 4
HEAD_SIZE = 64
GROUP = QUERY_HEADS // KEY_HEADS
POSITIONS = 8
ROWS = GROUP * POSITIONS
WIDTH = KEY_HEADS * HEAD_SIZE
MESSAGE = WIDTH + 128

LOWEST = float(jnp.bfloat16(-1e30))
DEAD_MARK = 64.0

F32 = jnp.float32
BF16 = jnp.bfloat16
VMEM_LIMIT = 48 * 1024 * 1024


def head_of_lane(shape):
    return lax.broadcasted_iota(jnp.int32, shape, len(shape) - 1) // HEAD_SIZE


def swap_halves(x):
    pieces = [pltpu.roll(x[:, i : i + 128], HEAD_SIZE, 1) for i in range(0, x.shape[1], 128)]
    return jnp.concatenate(pieces, axis=1)


def spread_queries(q):
    lanes = head_of_lane(q.shape)
    zero = jnp.zeros_like(q)
    return jnp.concatenate([jnp.where(lanes == c, q, zero) for c in range(KEY_HEADS)], axis=0)


def fold_heads(x):
    lanes = head_of_lane((ROWS, WIDTH))
    out = jnp.broadcast_to(x[:ROWS], (ROWS, WIDTH))
    for c in range(1, KEY_HEADS):
        out = jnp.where(lanes == c, x[c * ROWS : (c + 1) * ROWS], out)
    return out


def score(q, keys):
    return lax.dot_general(
        spread_queries(q), keys, (((1,), (1,)), ((), ())), preferred_element_type=F32
    )


def weigh(weights, values):
    ones = jnp.ones((values.shape[0], 128), BF16)
    mass = jnp.dot(weights, ones, preferred_element_type=F32)
    part = jnp.dot(weights, values, preferred_element_type=F32)
    return jnp.concatenate([mass, mass], axis=1), part


def attend(q, keys, values, live):
    masked = jnp.where(live, score(q, keys), LOWEST)
    top = jnp.max(masked, axis=1, keepdims=True)
    weights = jnp.exp(masked - top).astype(BF16)
    mass, part = weigh(weights, values)
    return fold_heads(top), fold_heads(mass), fold_heads(part)


def attend_two(q, keys, values, live):
    masked = jnp.where(live, score(q, keys), LOWEST)
    first = lax.broadcasted_iota(jnp.int32, masked.shape, 1) < masked.shape[1] // 2
    top_a = jnp.max(jnp.where(first, masked, LOWEST), axis=1, keepdims=True)
    top_b = jnp.max(jnp.where(first, LOWEST, masked), axis=1, keepdims=True)
    weights = jnp.exp(masked - jnp.where(first, top_a, top_b))
    both = jnp.concatenate(
        [jnp.where(first, weights, 0.0), jnp.where(first, 0.0, weights)], axis=0
    ).astype(BF16)
    mass, part = weigh(both, values)
    rows = masked.shape[0]
    return (
        (fold_heads(top_a), fold_heads(mass[:rows]), fold_heads(part[:rows])),
        (fold_heads(top_b), fold_heads(mass[rows:]), fold_heads(part[rows:])),
    )


def merge(*blocks):
    top = functools.reduce(jnp.maximum, [b[0] for b in blocks])
    lifts = [jnp.exp(b[0] - top) for b in blocks]
    mass = functools.reduce(jnp.add, [a * b[1] for a, b in zip(lifts, blocks)])
    part = functools.reduce(jnp.add, [a * b[2] for a, b in zip(lifts, blocks)])
    return top, mass, part


def pack_message(top, mass, part):
    rounded = top.astype(BF16).astype(F32)
    lift = jnp.exp(top - rounded)
    top, mass, part = rounded, mass * lift, part * lift
    lane = lax.broadcasted_iota(jnp.int32, (ROWS, 128), 1)
    first = (lane % 64) < 32
    narrow = lambda x: jnp.where(first, x[:, :128], x[:, 128:])
    top, mass = narrow(top), narrow(mass)
    high = mass.astype(BF16).astype(F32)
    place = lane % 32
    packed = jnp.where(
        place == 0, top, jnp.where(place == 1, high, jnp.where(place == 2, mass - high, 0.0))
    )
    return part, packed


def open_message(message):
    row = lax.broadcasted_iota(jnp.int32, (128, WIDTH), 0)
    head = lax.broadcasted_iota(jnp.int32, (128, WIDTH), 1) // HEAD_SIZE
    owner = ((row // 32) % 2) * 2 + row // 64
    place = row % 32
    pick_top = jnp.where((owner == head) & (place == 0), 1.0, 0.0).astype(BF16)
    pick_mass = jnp.where((owner == head) & ((place == 1) | (place == 2)), 1.0, 0.0).astype(BF16)
    packed = message[:, WIDTH:].astype(BF16)
    top = jnp.dot(packed, pick_top, preferred_element_type=F32)
    mass = jnp.dot(packed, pick_mass, preferred_element_type=F32)
    return top, mass, message[:, :WIDTH]


def start_copies(pairs, sems):
    copies = [
        pltpu.make_async_copy(source, target, sems.at[i]) for i, (source, target) in enumerate(pairs)
    ]
    for copy in copies:
        copy.start()
    return copies


def prompts_out_kernel(mask_hbm, keys_hbm, values_hbm, out_ref, mask_ref, sems):
    held, rows = keys_hbm.shape[0], keys_hbm.shape[1]
    copies = start_copies(
        [
            (mask_hbm, mask_ref),
            (keys_hbm, out_ref.at[:, pl.ds(0, rows)]),
            (values_hbm, out_ref.at[:, pl.ds(rows, rows)]),
        ],
        sems,
    )
    for copy in copies:
        copy.wait()
    at = lax.broadcasted_iota(jnp.int32, (16, 128), 0) + lax.broadcasted_iota(
        jnp.int32, (16, 128), 1
    )
    for i in range(held):
        dead = mask_ref[0, i] != 1
        keys = out_ref[i, :16, :128].astype(F32)
        out_ref[i, :16, :128] = jnp.where((at == 0) & dead, DEAD_MARK, keys).astype(BF16)


def queries_out_kernel(own_ref, sibling_ref, out_ref, pad_ref):
    count, each = own_ref.shape[1], own_ref.shape[2]
    low = lax.broadcasted_iota(jnp.int32, (POSITIONS, 128), 1) < HEAD_SIZE
    pad_ref[...] = jnp.zeros_like(pad_ref)
    for i in range(2 * each):
        source = own_ref if i < each else sibling_ref
        for n in range(count):
            pad_ref[i, n : n + 1] = source[0, n].astype(F32)[i % each : i % each + 1]
    for i in range(2 * each):
        q = pad_ref[i] * HEAD_SIZE**-0.5
        swapped = swap_halves(q)
        rows = []
        for g in range(GROUP):
            columns = []
            for c in range(0, KEY_HEADS, 2):
                halves = []
                for half in range(2):
                    tile = (GROUP * (c + half) + g) // 2
                    array = q if g % 2 == half else swapped
                    halves.append(array[:, tile * 128 : tile * 128 + 128])
                columns.append(jnp.where(low, halves[0], halves[1]))
            rows.append(jnp.concatenate(columns, axis=1))
        out_ref[i] = jnp.concatenate(rows, axis=0).astype(BF16)


def place_of(request, each, chip, core, kept):
    device = lax.div(request, each)
    distance = lax.shift_right_logical(device, 1) ^ chip
    return ((device & 1) ^ core) * kept + distance * each + lax.rem(request, each)


def own_kernel(chips, each, shifts, held, *refs):
    owner_hbm, length_hbm, accepted_hbm, group_hbm = refs[:4]
    pk_hbm, nk_hbm, pv_hbm, nv_hbm, keys_hbm, values_hbm = refs[4:10]
    query_ref, own_out, table_out, keys_out, values_out = refs[10:15]
    owner_ref, length_ref, accepted_ref, group_ref, owner_row, near, rows_ref = refs[15:22]
    small_sems, near_sems, key_sems, value_sems = refs[22:]
    pieces, rows = keys_out.shape[0], keys_out.shape[1]
    kept = chips * each
    small = start_copies(
        [
            (owner_hbm, owner_ref),
            (length_hbm, length_ref),
            (accepted_hbm, accepted_ref),
            (group_hbm, group_ref),
            (owner_hbm, owner_row),
        ],
        small_sems,
    )
    small += start_copies(
        [(x.at[0], near.at[j]) for j, x in enumerate((pk_hbm, nk_hbm, pv_hbm, nv_hbm))], near_sems
    )
    large = start_copies([(keys_hbm.at[0, i], keys_out.at[i]) for i in range(pieces)], key_sems)
    large += start_copies([(values_hbm.at[0, i], values_out.at[i]) for i in range(pieces)], value_sems)
    me = lax.axis_index("blk")
    z = lax.axis_index("req")
    chip, core = lax.shift_right_logical(me, 1), me & 1
    rows_ref[...] = jnp.zeros_like(rows_ref)
    for copy in small:
        copy.wait()

    count = near.shape[1]
    for n in range(count):
        for j in range(4):
            pair = near[j, n].astype(F32)
            for k in range(each):
                at = (j % 2) * POSITIONS + n
                rows_ref[j // 2, k, at : at + 1] = pair[k : k + 1]
    for k in range(each):
        shape = (KEY_HEADS * ROWS, 2 * POSITIONS)
        column = lax.broadcasted_iota(jnp.int32, shape, 1)
        position = lax.broadcasted_iota(jnp.int32, shape, 0) % POSITIONS
        taken = accepted_ref[0, k]
        live = ((column < POSITIONS) & (column < taken)) | (
            (column >= POSITIONS)
            & (column < POSITIONS + count)
            & (column - POSITIONS <= position)
        )
        got = attend(query_ref[k], rows_ref[0, k].astype(BF16), rows_ref[1, k].astype(BF16), live)
        for j in range(3):
            own_out[j, k] = got[j]

    owners = owner_row[...]
    slot = lax.broadcasted_iota(jnp.int32, owners.shape, 1)
    for i in range(pieces):
        index = me * pieces + i
        owner = owner_ref[0, index]
        same = jnp.where((owners == owner) & (slot < index), 1.0, 0.0)
        rank = jnp.sum(same, axis=1, keepdims=True).astype(jnp.int32)
        place = place_of(owner, each, chip, core, kept)
        table_out[i : i + 1] = jnp.full((1, 128), place, jnp.int32)
        table_out[pieces + i : pieces + i + 1] = jnp.broadcast_to(
            length_ref[0, owner] - rank * rows, (1, 128)
        )
    for i in range(kept):
        request = ((chip ^ (i // each)) * 2 + core) * each + i % each
        group = group_ref[0, request]
        shift = lax.rem(z - lax.div(group, held) + shifts, shifts)
        at = shift * held + lax.rem(group, held)
        table_out[2 * pieces + i : 2 * pieces + i + 1] = jnp.full((1, 128), at, jnp.int32)
    for copy in large:
        copy.wait()


def pieces_kernel(chips, each, *refs):
    table_ref, own_ref = refs[:2]
    query_refs = refs[2 : 2 + chips]
    keys, values, mine_out, sibling_out, queries, acc = refs[2 + chips :]
    pieces, rows = keys.shape[0], keys.shape[1]
    kept = chips * each
    for s in range(chips):
        for side in range(2):
            queries[side * kept + s * each : side * kept + (s + 1) * each] = query_refs[s][
                side * each : (side + 1) * each
            ]
    lane = lax.broadcasted_iota(jnp.int32, (1, rows), 1)
    places = [jnp.max(table_ref[i : i + 1]) for i in range(pieces)]
    got = []
    for i in range(pieces):
        filled = table_ref[pieces + i : pieces + i + 1]
        live = lane < jnp.concatenate([filled] * (rows // 128), axis=1)
        got.append(attend(queries[places[i]], keys[i], values[i], live))
    acc[0] = jnp.full_like(acc[0], LOWEST)
    acc[1] = jnp.zeros_like(acc[1])
    acc[2] = jnp.zeros_like(acc[2])
    for k in range(each):
        acc[0, k] = own_ref[0, k]
    for i in range(pieces):
        acc[0, places[i]] = jnp.maximum(acc[0, places[i]], got[i][0])
    for k in range(each):
        lift = jnp.exp(own_ref[0, k] - acc[0, k])
        acc[1, k] = own_ref[1, k] * lift
        acc[2, k] = own_ref[2, k] * lift
    for i in range(pieces):
        lift = jnp.exp(got[i][0] - acc[0, places[i]])
        acc[1, places[i]] += lift * got[i][1]
        acc[2, places[i]] += lift * got[i][2]
    mine_out[...] = acc[:, :kept]
    sibling_out[...] = acc[:, kept:]


def join_kernel(mine_ref, sibling_ref, out_ref):
    for i in range(mine_ref.shape[1]):
        joined = merge([mine_ref[j, i] for j in range(3)], [sibling_ref[j, i] for j in range(3)])
        for j in range(3):
            out_ref[j, i] = joined[j]


def prompts_kernel(chips, each, shifts, first_row, *refs):
    table_ref = refs[0]
    query_refs = refs[1 : 1 + chips]
    joined_ref = refs[1 + chips]
    block_refs = refs[2 + chips : 2 + chips + 2 * shifts]
    out_refs = refs[2 + chips + 2 * shifts :]
    held, rows = block_refs[0].shape[0], block_refs[0].shape[1] // 2
    lane = lax.broadcasted_iota(jnp.int32, (1, 2 * rows), 1)
    got = []
    for i in range(chips * each):
        at = jnp.max(table_ref[first_row + i : first_row + i + 1])
        shift, slot = lax.div(at, held), lax.rem(at, held)

        def block(side):
            out = block_refs[side * shifts][slot]
            for s in range(1, shifts):
                out = jnp.where(shift == s, block_refs[side * shifts + s][slot], out)
            return out

        mine, other = block(0), block(1)
        marks = jnp.where(lane < rows, mine[:1, :1].astype(F32), other[:1, :1].astype(F32))
        got.append(
            attend_two(
                query_refs[i // each][i % each],
                jnp.concatenate([mine[:rows], other[:rows]], axis=0),
                jnp.concatenate([mine[rows:], other[rows:]], axis=0),
                marks < 0.5 * DEAD_MARK,
            )
        )
    for i in range(chips * each):
        merged = merge([joined_ref[j, i] for j in range(3)], *got[i])
        part, packed = pack_message(*merged)
        out_refs[i // each][i % each, :, :WIDTH] = part
        out_refs[i // each][i % each, :, WIDTH:] = packed


def combine_kernel(chips, *refs):
    message_refs, out_ref = refs[:chips], refs[chips]
    count, each = out_ref.shape[1], out_ref.shape[2]
    low = lax.broadcasted_iota(jnp.int32, (POSITIONS, 128), 1) < HEAD_SIZE
    rows = []
    for k in range(each):
        parts = [open_message(ref[k]) for ref in message_refs]
        _, mass, part = merge(*parts)
        out = part / mass
        swapped = swap_halves(out)
        columns = []
        for head in range(0, QUERY_HEADS, 2):
            c, g = head // GROUP, head % GROUP
            tile = slice((c // 2) * 128, (c // 2) * 128 + 128)
            first, second = (out, swapped) if c % 2 == 0 else (swapped, out)
            columns.append(
                jnp.where(
                    low,
                    first[g * POSITIONS : (g + 1) * POSITIONS, tile],
                    second[(g + 1) * POSITIONS : (g + 2) * POSITIONS, tile],
                )
            )
        rows.append(jnp.concatenate(columns, axis=1))
    for n in range(count):
        out_ref[0, n] = jnp.concatenate([row[n : n + 1] for row in rows], axis=0).astype(BF16)


HBM = pl.BlockSpec(memory_space=pltpu.HBM)
VMEM = pl.BlockSpec(memory_space=pltpu.VMEM)


def in_hbm(x):
    return pltpu.with_memory_space_constraint(x, pltpu.HBM)


def call(kernel, name, out_shape, in_specs, scratch=(), cost=0):
    many = isinstance(out_shape, (list, tuple))
    return pl.pallas_call(
        kernel,
        name=name,
        out_shape=out_shape,
        in_specs=in_specs,
        out_specs=[VMEM] * len(out_shape) if many else VMEM,
        scratch_shapes=list(scratch),
        cost_estimate=pl.CostEstimate(flops=0, bytes_accessed=cost, transcendentals=0),
        compiler_params=pltpu.CompilerParams(vmem_limit_bytes=VMEM_LIMIT),
    )


def per_device(
    devices,
    shifts,
    verified_queries,
    new_keys,
    verified_value_rows,
    prior_round_keys,
    prior_round_values,
    accepted,
    group_id,
    cache_len,
    slot_owner,
    piece_cache_keys,
    piece_cache_values,
    shared_prompt_keys,
    shared_prompt_values,
    prompt_mask,
):
    shape = jax.ShapeDtypeStruct
    each = verified_queries.shape[1]
    chips = devices // 2
    pieces, piece_rows = piece_cache_keys.shape[1:3]
    held, block_rows = shared_prompt_keys.shape[:2]
    kept = chips * each

    def other_core(x):
        return lax.ppermute(x, "blk", [(i, i ^ 1) for i in range(devices)])

    def other_chip(x, s):
        return lax.ppermute(x, "blk", [(i, i ^ (2 * s)) for i in range(devices)])

    def along_req(x, s):
        return lax.ppermute(x, "req", [(i, (i + s) % shifts) for i in range(shifts)])

    verified_queries, prior_round_keys, new_keys, prior_round_values, verified_value_rows = (
        jnp.transpose(x, (0, 2, 1, 3))
        for x in (
            verified_queries, prior_round_keys, new_keys, prior_round_values, verified_value_rows,
        )
    )
    sibling_queries = other_core(verified_queries)
    own_blocks = call(
        prompts_out_kernel,
        "prompts_out",
        shape((held, 2 * block_rows, WIDTH), BF16),
        [HBM] * 3,
        [pltpu.SMEM((1, held), jnp.int32), pltpu.SemaphoreType.DMA((3,))],
    )(in_hbm(prompt_mask.T), in_hbm(shared_prompt_keys), in_hbm(shared_prompt_values))
    blocks = [own_blocks] + [along_req(own_blocks, s) for s in range(1, shifts)]

    sibling_queries, own_blocks = lax.optimization_barrier((sibling_queries, own_blocks))
    chip_queries = call(
        queries_out_kernel,
        "queries_out",
        shape((2 * each, ROWS, WIDTH), BF16),
        [VMEM, VMEM],
        [pltpu.VMEM((2 * each, POSITIONS, QUERY_HEADS * HEAD_SIZE), F32)],
    )(verified_queries, sibling_queries)
    queries = [chip_queries] + [other_chip(chip_queries, s) for s in range(1, chips)]

    near = (prior_round_keys, new_keys, prior_round_values, verified_value_rows)
    count = verified_queries.shape[1]
    piece_shape = (pieces, piece_rows, WIDTH)
    own, table, keys, values = call(
        functools.partial(own_kernel, chips, each, shifts, held),
        "own",
        [
            shape((3, each, ROWS, WIDTH), F32),
            shape((2 * pieces + kept, 128), jnp.int32),
            shape(piece_shape, BF16),
            shape(piece_shape, BF16),
        ],
        [HBM] * 10 + [VMEM],
        [
            pltpu.SMEM(slot_owner.shape, jnp.int32),
            pltpu.SMEM(cache_len.shape, jnp.int32),
            pltpu.SMEM(accepted.shape, jnp.int32),
            pltpu.SMEM(group_id.shape, jnp.int32),
            pltpu.VMEM(slot_owner.shape, jnp.int32),
            pltpu.VMEM((4, count, each, WIDTH), BF16),
            pltpu.VMEM((2, each, 2 * POSITIONS, WIDTH), F32),
            pltpu.SemaphoreType.DMA((5,)),
            pltpu.SemaphoreType.DMA((4,)),
            pltpu.SemaphoreType.DMA((pieces,)),
            pltpu.SemaphoreType.DMA((pieces,)),
        ],
        8 * 1024 * 1024,
    )(
        *(in_hbm(x) for x in (slot_owner, cache_len, accepted, group_id) + near),
        in_hbm(piece_cache_keys),
        in_hbm(piece_cache_values),
        chip_queries,
    )

    wide = (kept, ROWS, WIDTH)
    mine, to_sibling = call(
        functools.partial(pieces_kernel, chips, each),
        "pieces",
        [shape((3,) + wide, F32)] * 2,
        [VMEM] * (chips + 4),
        [
            pltpu.VMEM((2 * kept, ROWS, WIDTH), BF16),
            pltpu.VMEM((3, 2 * kept, ROWS, WIDTH), F32),
        ],
    )(table, own, *queries, keys, values)
    to_sibling, *blocks = lax.optimization_barrier((to_sibling, *blocks))
    joined = call(join_kernel, "join", shape((3,) + wide, F32), [VMEM, VMEM])(
        mine, other_core(to_sibling)
    )
    sibling_blocks = [other_core(x) for x in blocks]

    messages = call(
        functools.partial(prompts_kernel, chips, each, shifts, 2 * pieces),
        "prompts",
        [shape((each, ROWS, MESSAGE), F32)] * chips,
        [VMEM] * (2 + chips + 2 * shifts),
    )(table, *queries, joined, *blocks, *sibling_blocks)
    arrived = [messages[0]] + [other_chip(messages[s], s) for s in range(1, chips)]

    out = call(
        functools.partial(combine_kernel, chips),
        "combine",
        shape(verified_queries.shape, BF16),
        [VMEM] * chips,
    )(*arrived)
    return jnp.transpose(out, (0, 2, 1, 3))


def solution(mesh):
    placed = (
        P("req", "blk", None, None),
        P("req", "blk", None, None),
        P("req", "blk", None, None),
        P("req", "blk", None, None),
        P("req", "blk", None, None),
        P("req", "blk"),
        P("req", None),
        P("req", None),
        P("req", None),
        P("req", "blk", None, None),
        P("req", "blk", None, None),
        P("req", "blk", None),
        P("req", "blk", None),
        P("req", "blk"),
    )
    return jax.shard_map(
        functools.partial(per_device, mesh.shape["blk"], mesh.shape["req"]),
        mesh=mesh,
        in_specs=placed,
        out_specs=P("req", "blk", None, None),
        check_vma=False,
    )
```

```python
import functools

import jax
import jax.numpy as jnp
from jax import lax
from jax.experimental import pallas as pl
from jax.experimental.pallas import tpu as pltpu
from jax.sharding import PartitionSpec as P

QUERY_HEADS = 16
KEY_HEADS = 4
HEAD_SIZE = 64
GROUP = QUERY_HEADS // KEY_HEADS
POSITIONS = 8
ROWS = GROUP * POSITIONS
WIDTH = KEY_HEADS * HEAD_SIZE
MESSAGE = 3 * POSITIONS

LOWEST = float(jnp.bfloat16(-1e30))
DEAD_MARK = 64.0

F32 = jnp.float32
BF16 = jnp.bfloat16
VMEM_LIMIT = 48 * 1024 * 1024


def head_of_lane(shape):
    return lax.broadcasted_iota(jnp.int32, shape, len(shape) - 1) // HEAD_SIZE


def swap_halves(x):
    pieces = [pltpu.roll(x[:, i : i + 128], HEAD_SIZE, 1) for i in range(0, x.shape[1], 128)]
    return jnp.concatenate(pieces, axis=1)


def spread_queries(q):
    lanes = head_of_lane(q.shape)
    zero = jnp.zeros_like(q)
    return jnp.concatenate([jnp.where(lanes == c, q, zero) for c in range(KEY_HEADS)], axis=0)


def fold_heads(x):
    lanes = head_of_lane((ROWS, WIDTH))
    out = jnp.broadcast_to(x[:ROWS], (ROWS, WIDTH))
    for c in range(1, KEY_HEADS):
        out = jnp.where(lanes == c, x[c * ROWS : (c + 1) * ROWS], out)
    return out


def score(q, keys):
    return lax.dot_general(
        spread_queries(q), keys, (((1,), (1,)), ((), ())), preferred_element_type=F32
    )


def weigh(weights, values):
    ones = jnp.ones((values.shape[0], 128), BF16)
    mass = jnp.dot(weights, ones, preferred_element_type=F32)
    part = jnp.dot(weights, values, preferred_element_type=F32)
    return jnp.concatenate([mass, mass], axis=1), part


def attend(q, keys, values, live):
    masked = jnp.where(live, score(q, keys), LOWEST)
    top = jnp.max(masked, axis=1, keepdims=True)
    weights = jnp.exp(masked - top).astype(BF16)
    mass, part = weigh(weights, values)
    return fold_heads(top), fold_heads(mass), fold_heads(part)


def attend_two(q, keys, values, live):
    masked = jnp.where(live, score(q, keys), LOWEST)
    first = lax.broadcasted_iota(jnp.int32, masked.shape, 1) < masked.shape[1] // 2
    top_a = jnp.max(jnp.where(first, masked, LOWEST), axis=1, keepdims=True)
    top_b = jnp.max(jnp.where(first, LOWEST, masked), axis=1, keepdims=True)
    weights = jnp.exp(masked - jnp.where(first, top_a, top_b))
    both = jnp.concatenate(
        [jnp.where(first, weights, 0.0), jnp.where(first, 0.0, weights)], axis=0
    ).astype(BF16)
    mass, part = weigh(both, values)
    rows = masked.shape[0]
    return (
        (fold_heads(top_a), fold_heads(mass[:rows]), fold_heads(part[:rows])),
        (fold_heads(top_b), fold_heads(mass[rows:]), fold_heads(part[rows:])),
    )


def merge(*blocks):
    top = functools.reduce(jnp.maximum, [b[0] for b in blocks])
    lifts = [jnp.exp(b[0] - top) for b in blocks]
    mass = functools.reduce(jnp.add, [a * b[1] for a, b in zip(lifts, blocks)])
    part = functools.reduce(jnp.add, [a * b[2] for a, b in zip(lifts, blocks)])
    return top, mass, part


def spot(shape):
    lane = lax.broadcasted_iota(jnp.int32, shape, 1) % HEAD_SIZE
    return lane == lax.broadcasted_iota(jnp.int32, shape, 0) % ROWS


def pack_message(top, mass, part):
    rounded = top.astype(BF16).astype(F32)
    lift = jnp.exp(top - rounded)
    mass, part = mass * lift, part * lift
    high = mass.astype(BF16).astype(F32)
    at = spot((ROWS, WIDTH))
    row_of = lambda x: jnp.sum(jnp.where(at, x, 0.0), axis=0, keepdims=True)
    sub = lax.broadcasted_iota(jnp.int32, (POSITIONS, WIDTH), 0)
    tile = lambda i: part[i * POSITIONS : (i + 1) * POSITIONS]
    return jnp.concatenate(
        [
            jnp.where(sub < 5, tile(0), pltpu.roll(tile(3), 5, 0)),
            jnp.where(sub < 5, tile(1), jnp.where(sub < 7, pltpu.roll(tile(3), 2, 0), row_of(rounded))),
            jnp.where(sub < 5, tile(2), jnp.where(sub < 6, row_of(high), row_of(mass - high))),
        ],
        axis=0,
    )


def open_messages(messages):
    at = spot((ROWS, WIDTH))
    rows = []
    for x in messages:
        for r in (15, 21, 22):
            rows.append(jnp.where(at, x[r : r + 1], 0.0).astype(BF16))
    same_head = lax.broadcasted_iota(jnp.int32, (WIDTH, WIDTH), 0) // HEAD_SIZE == (
        lax.broadcasted_iota(jnp.int32, (WIDTH, WIDTH), 1) // HEAD_SIZE
    )
    ones = jnp.where(same_head, 1.0, 0.0).astype(BF16)
    spread = jnp.dot(jnp.concatenate(rows, axis=0), ones, preferred_element_type=F32)
    sub = lax.broadcasted_iota(jnp.int32, (POSITIONS, WIDTH), 0)
    out = []
    for i, x in enumerate(messages):
        get = lambda j: spread[(3 * i + j) * ROWS : (3 * i + j + 1) * ROWS]
        last = jnp.where(sub < 3, pltpu.roll(x[0:8], 3, 0), pltpu.roll(x[8:16], 6, 0))
        out.append((get(0), get(1) + get(2), jnp.concatenate([x, last], axis=0)))
    return out


def start_copies(pairs, sems):
    copies = [
        pltpu.make_async_copy(source, target, sems.at[i]) for i, (source, target) in enumerate(pairs)
    ]
    for copy in copies:
        copy.start()
    return copies


def format_queries(q):
    low = lax.broadcasted_iota(jnp.int32, (POSITIONS, 128), 1) < HEAD_SIZE
    swapped = swap_halves(q)
    rows = []
    for g in range(GROUP):
        columns = []
        for c in range(0, KEY_HEADS, 2):
            halves = []
            for half in range(2):
                tile = (GROUP * (c + half) + g) // 2
                array = q if g % 2 == half else swapped
                halves.append(array[:, tile * 128 : tile * 128 + 128])
            columns.append(jnp.where(low, halves[0], halves[1]))
        rows.append(jnp.concatenate(columns, axis=1))
    return jnp.concatenate(rows, axis=0)


def across_cores(j, chips):
    if j == 0 or j == chips - 1:
        return j
    return j + 1 if j % 2 else j - 1


def place_of(request, each, chip, core, kept):
    device = lax.div(request, each)
    distance = lax.shift_right_logical(device, 1) ^ chip
    return ((device & 1) ^ core) * kept + distance * each + lax.rem(request, each)


def parcel_kernel(mask_hbm, keys_hbm, values_hbm, query_hbm, parcel, mask_ref, query, pad, sems):
    held, rows = keys_hbm.shape[:2]
    pairs = [(mask_hbm, mask_ref), (query_hbm, query)]
    for i in range(held):
        at = 2 * i * rows
        pairs.append((keys_hbm.at[i], parcel.at[pl.ds(at, rows)]))
        pairs.append((values_hbm.at[i], parcel.at[pl.ds(at + rows, rows)]))
    copies = start_copies(pairs, sems)
    pad[...] = jnp.zeros_like(pad)
    for copy in copies:
        copy.wait()
    at = lax.broadcasted_iota(jnp.int32, (16, 128), 0) + lax.broadcasted_iota(
        jnp.int32, (16, 128), 1
    )
    for i in range(held):
        spot_rows = slice(2 * i * rows, 2 * i * rows + 16)
        keys = parcel[spot_rows, :128].astype(F32)
        dead = mask_ref[0, i] != 1
        parcel[spot_rows, :128] = jnp.where((at == 0) & dead, DEAD_MARK, keys).astype(BF16)
    count, each = query.shape[1:3]
    for n in range(count):
        pair = query[0, n].astype(F32) * HEAD_SIZE**-0.5
        for k in range(each):
            pad[k, n : n + 1] = pair[k : k + 1]
    end = 2 * held * rows
    for k in range(each):
        parcel[end + k * ROWS : end + (k + 1) * ROWS] = format_queries(pad[k]).astype(BF16)


def own_kernel(chips, each, shifts, held, *refs):
    owner_hbm, length_hbm, accepted_hbm, group_hbm = refs[:4]
    near_hbm, (keys_hbm, values_hbm) = refs[4:8], refs[8:10]
    query_ref, own_out, table_out, keys_out, values_out = refs[10:15]
    owner_ref, length_ref, accepted_ref, group_ref = refs[15:19]
    owner_row, near, rows_ref, small_sems, piece_sems = refs[19:]
    pieces, rows = keys_out.shape[:2]
    kept = chips * each
    small = start_copies(
        [
            (owner_hbm, owner_ref),
            (length_hbm, length_ref),
            (accepted_hbm, accepted_ref),
            (group_hbm, group_ref),
            (owner_hbm, owner_row),
        ]
        + [(x.at[0], near.at[j]) for j, x in enumerate(near_hbm)],
        small_sems,
    )
    large = start_copies(
        [(keys_hbm.at[0, i], keys_out.at[i]) for i in range(pieces)]
        + [(values_hbm.at[0, i], values_out.at[i]) for i in range(pieces)],
        piece_sems,
    )
    me = lax.axis_index("blk")
    z = lax.axis_index("req")
    chip, core = lax.shift_right_logical(me, 1), me & 1
    rows_ref[...] = jnp.zeros_like(rows_ref)
    for copy in small:
        copy.wait()
    count = near.shape[1]
    for n in range(count):
        for j in range(4):
            pair = near[j, n].astype(F32)
            for k in range(each):
                to = (j % 2) * POSITIONS + n
                rows_ref[j // 2, k, to : to + 1] = pair[k : k + 1]

    shape = (KEY_HEADS * ROWS, 2 * POSITIONS)
    column = lax.broadcasted_iota(jnp.int32, shape, 1)
    position = lax.broadcasted_iota(jnp.int32, shape, 0) % POSITIONS
    for k in range(each):
        live = ((column < POSITIONS) & (column < accepted_ref[0, k])) | (
            (column >= POSITIONS)
            & (column < POSITIONS + count)
            & (column - POSITIONS <= position)
        )
        got = attend(query_ref[k], rows_ref[0, k].astype(BF16), rows_ref[1, k].astype(BF16), live)
        for j in range(3):
            own_out[j, k] = got[j]

    owners = owner_row[...]
    slot = lax.broadcasted_iota(jnp.int32, owners.shape, 1)
    for i in range(pieces):
        index = me * pieces + i
        owner = owner_ref[0, index]
        same = jnp.where((owners == owner) & (slot < index), 1.0, 0.0)
        rank = jnp.sum(same, axis=1, keepdims=True).astype(jnp.int32)
        place = place_of(owner, each, chip, core, kept)
        table_out[i : i + 1] = jnp.full((1, 128), place, jnp.int32)
        table_out[pieces + i : pieces + i + 1] = jnp.broadcast_to(
            length_ref[0, owner] - rank * rows, (1, 128)
        )
    for i in range(kept):
        request = ((chip ^ (i // each)) * 2 + core) * each + i % each
        group = group_ref[0, request]
        shift = z ^ lax.div(group, held)
        fetched = (shift & ~1) - 1 + ((shift ^ core) & 1)
        array = jnp.where(shift == 0, 0, jnp.where(shift == 1, shifts - 1, fetched))
        to = 2 * pieces + i
        table_out[to : to + 1] = jnp.full((1, 128), array * held + lax.rem(group, held), jnp.int32)
    for copy in large:
        copy.wait()


def pair_kernel(own_ref, sibling_ref, both_ref, own_blocks_ref, queries_ref):
    held, size = own_blocks_ref.shape[:2]
    half = queries_ref.shape[0] // 2
    for side, ref in enumerate((own_ref, sibling_ref)):
        for i in range(held):
            block = ref[i * size : (i + 1) * size]
            both_ref[side * held + i] = block
            if side == 0:
                own_blocks_ref[i] = block
        for k in range(half):
            at = held * size + k * ROWS
            queries_ref[side * half + k] = ref[at : at + ROWS]


def pieces_kernel(chips, each, *refs):
    table_ref = refs[0]
    query_refs = refs[1 : 1 + chips]
    keys, values, mine_out = refs[1 + chips : 4 + chips]
    sibling_outs = refs[4 + chips : 6 + chips]
    queries_out, queries, acc = refs[6 + chips :]
    pieces, rows = keys.shape[0], keys.shape[1]
    kept = chips * each
    core = lax.axis_index("blk") & 1
    for j in range(chips):
        distance = jnp.where(core == 0, j, across_cores(j, chips))
        handed = j > 0 and j < chips - 1 and j % 2 == 0
        for side in range(2):
            start = (1 - side if handed else side) * each
            queries[pl.ds(side * kept + distance * each, each)] = query_refs[j][
                start : start + each
            ]
    queries_out[...] = queries[:kept]
    lane = lax.broadcasted_iota(jnp.int32, (1, rows), 1)
    places = [jnp.max(table_ref[i : i + 1]) for i in range(pieces)]
    got = []
    for i in range(pieces):
        filled = table_ref[pieces + i : pieces + i + 1]
        live = lane < jnp.concatenate([filled] * (rows // 128), axis=1)
        got.append(attend(queries[places[i]], keys[i], values[i], live))
    acc[0] = jnp.full_like(acc[0], LOWEST)
    acc[1] = jnp.zeros_like(acc[1])
    acc[2] = jnp.zeros_like(acc[2])
    for i in range(pieces):
        acc[0, places[i]] = jnp.maximum(acc[0, places[i]], got[i][0])
    for i in range(pieces):
        lift = jnp.exp(got[i][0] - acc[0, places[i]])
        acc[1, places[i]] += lift * got[i][1]
        acc[2, places[i]] += lift * got[i][2]
    mine_out[...] = acc[:, :kept]
    for i in range(kept):
        half, at = divmod(i, kept // 2)
        sibling_outs[half][at] = pack_message(*[acc[j, kept + i] for j in range(3)])


def join_kernel(mine_ref, own_ref, first_ref, second_ref, out_ref):
    half, each = first_ref.shape[0], own_ref.shape[1]
    opened = open_messages([first_ref[i] for i in range(half)] + [second_ref[i] for i in range(half)])
    for i in range(2 * half):
        blocks = [[mine_ref[j, i] for j in range(3)], opened[i]]
        if i < each:
            blocks.append([own_ref[j, i] for j in range(3)])
        joined = merge(*blocks)
        for j in range(3):
            out_ref[j, i] = joined[j]


def prompts_kernel(chips, each, shifts, first_row, *refs):
    table_ref, query_ref, joined_ref = refs[:3]
    array_refs, near_refs, out_refs = refs[3 : 2 + shifts], refs[2 + shifts : 4 + shifts], refs[4 + shifts :]
    held, rows = near_refs[0].shape[0], near_refs[0].shape[1] // 2
    lane = lax.broadcasted_iota(jnp.int32, (1, 2 * rows), 1)
    got = []
    for i in range(chips * each):
        at = jnp.max(table_ref[first_row + i : first_row + i + 1])
        array, slot = lax.div(at, held), lax.rem(at, held)

        def block(side):
            out = near_refs[side][slot]
            for j, ref in enumerate(array_refs):
                out = jnp.where(array == j, ref[side * held + slot], out)
            return out

        mine, other = block(0), block(1)
        marks = jnp.where(lane < rows, mine[:1, :1].astype(F32), other[:1, :1].astype(F32))
        got.append(
            attend(
                query_ref[i],
                jnp.concatenate([mine[:rows], other[:rows]], axis=0),
                jnp.concatenate([mine[rows:], other[rows:]], axis=0),
                marks < 0.5 * DEAD_MARK,
            )
        )
    for i in range(chips * each):
        merged = merge([joined_ref[j, i] for j in range(3)], got[i])
        out_refs[i // each][i % each] = pack_message(*merged)


def combine_kernel(chips, *refs):
    message_refs, out_ref = refs[:chips], refs[chips]
    count, each = out_ref.shape[1], out_ref.shape[2]
    low = lax.broadcasted_iota(jnp.int32, (POSITIONS, 128), 1) < HEAD_SIZE
    rows = []
    opened = open_messages([ref[k] for k in range(each) for ref in message_refs])
    for k in range(each):
        _, mass, part = merge(*opened[k * chips : (k + 1) * chips])
        out = part / mass
        swapped = swap_halves(out)
        columns = []
        for head in range(0, QUERY_HEADS, 2):
            c, g = head // GROUP, head % GROUP
            tile = slice((c // 2) * 128, (c // 2) * 128 + 128)
            first, second = (out, swapped) if c % 2 == 0 else (swapped, out)
            columns.append(
                jnp.where(
                    low,
                    first[g * POSITIONS : (g + 1) * POSITIONS, tile],
                    second[(g + 1) * POSITIONS : (g + 2) * POSITIONS, tile],
                )
            )
        rows.append(jnp.concatenate(columns, axis=1))
    for n in range(count):
        out_ref[0, n] = jnp.concatenate([row[n : n + 1] for row in rows], axis=0).astype(BF16)


ANY = pl.BlockSpec(memory_space=pl.ANY)
HBM = pl.BlockSpec(memory_space=pltpu.HBM)
VMEM = pl.BlockSpec(memory_space=pltpu.VMEM)


def in_hbm(x):
    return pltpu.with_memory_space_constraint(x, pltpu.HBM)


def call(kernel, name, out_shape, in_specs, scratch=(), cost=0):
    many = isinstance(out_shape, (list, tuple))
    return pl.pallas_call(
        kernel,
        name=name,
        out_shape=out_shape,
        in_specs=in_specs,
        out_specs=[VMEM] * len(out_shape) if many else VMEM,
        scratch_shapes=list(scratch),
        cost_estimate=pl.CostEstimate(flops=0, bytes_accessed=cost, transcendentals=0),
        compiler_params=pltpu.CompilerParams(vmem_limit_bytes=VMEM_LIMIT),
    )


def per_device(
    devices,
    shifts,
    verified_queries,
    new_keys,
    verified_value_rows,
    prior_round_keys,
    prior_round_values,
    accepted,
    group_id,
    cache_len,
    slot_owner,
    piece_cache_keys,
    piece_cache_values,
    shared_prompt_keys,
    shared_prompt_values,
    prompt_mask,
):
    shape = jax.ShapeDtypeStruct
    each = verified_queries.shape[1]
    chips = devices // 2
    pieces, piece_rows = piece_cache_keys.shape[1:3]
    held, block_rows = shared_prompt_keys.shape[:2]
    kept = chips * each

    def other_core(x):
        return lax.ppermute(x, "blk", [(i, i ^ 1) for i in range(devices)])

    def other_chip(x, s):
        return lax.ppermute(x, "blk", [(i, i ^ (2 * s)) for i in range(devices)])

    def along_req(x, even, odd):
        pairs = []
        for i in range(devices * shifts):
            d, z = divmod(i, shifts)
            pairs.append((i, d * shifts + (z ^ (odd if d % 2 else even))))
        return lax.ppermute(x, ("blk", "req"), pairs)

    verified_queries, prior_round_keys, new_keys, prior_round_values, verified_value_rows = (
        jnp.transpose(x, (0, 2, 1, 3))
        for x in (
            verified_queries, prior_round_keys, new_keys, prior_round_values, verified_value_rows,
        )
    )
    near = (prior_round_keys, new_keys, prior_round_values, verified_value_rows)
    count = verified_queries.shape[1]
    block_size = 2 * block_rows
    piece_shape = (pieces, piece_rows, WIDTH)
    parcel = call(
        parcel_kernel,
        "parcel",
        shape((held * block_size + each * ROWS, WIDTH), BF16),
        [HBM] * 4,
        [
            pltpu.SMEM((1, held), jnp.int32),
            pltpu.VMEM(verified_queries.shape, BF16),
            pltpu.VMEM((each, POSITIONS, QUERY_HEADS * HEAD_SIZE), F32),
            pltpu.SemaphoreType.DMA((2 + 2 * held,)),
        ],
    )(
        *(
            in_hbm(x)
            for x in (prompt_mask.T, shared_prompt_keys, shared_prompt_values, verified_queries)
        )
    )
    both_blocks, own_blocks, chip_queries = call(
        pair_kernel,
        "pair",
        [
            shape((2 * held, block_size, WIDTH), BF16),
            shape((held, block_size, WIDTH), BF16),
            shape((2 * each, ROWS, WIDTH), BF16),
        ],
        [VMEM] * 2,
    )(parcel, other_core(parcel))
    far_blocks = [along_req(both_blocks, s, s + 1) for s in range(2, shifts, 2)]
    near_blocks = along_req(own_blocks, 1, 1)

    own, table, keys, values = call(
        functools.partial(own_kernel, chips, each, shifts, held),
        "own",
        [
            shape((3, each, ROWS, WIDTH), F32),
            shape((2 * pieces + kept, 128), jnp.int32),
            shape(piece_shape, BF16),
            shape(piece_shape, BF16),
        ],
        [HBM] * 10 + [VMEM],
        [
            pltpu.SMEM(slot_owner.shape, jnp.int32),
            pltpu.SMEM(cache_len.shape, jnp.int32),
            pltpu.SMEM(accepted.shape, jnp.int32),
            pltpu.SMEM(group_id.shape, jnp.int32),
            pltpu.VMEM(slot_owner.shape, jnp.int32),
            pltpu.VMEM((4, count, each, WIDTH), BF16),
            pltpu.VMEM((2, each, 2 * POSITIONS, WIDTH), F32),
            pltpu.SemaphoreType.DMA((9,)),
            pltpu.SemaphoreType.DMA((2 * pieces,)),
        ],
        8 * 1024 * 1024,
    )(
        *(
            in_hbm(x)
            for x in (slot_owner, cache_len, accepted, group_id)
            + near
            + (piece_cache_keys, piece_cache_values)
        ),
        chip_queries,
    )

    queries = [chip_queries]
    for s in range(1, chips - 1, 2):
        fetched = lax.ppermute(
            chip_queries,
            "blk",
            [(i, i ^ (2 * (across_cores(s, chips) if i % 2 else s))) for i in range(devices)],
        )
        fetched = lax.optimization_barrier((fetched, table))[0]
        queries += [fetched, other_core(fetched)]
    if chips > 1:
        queries.append(other_chip(chip_queries, chips - 1))

    wide = (kept, ROWS, WIDTH)
    mine, *to_sibling, kept_queries = call(
        functools.partial(pieces_kernel, chips, each),
        "pieces",
        [shape((3,) + wide, F32)]
        + [shape((kept // 2, MESSAGE, WIDTH), F32)] * 2
        + [shape(wide, BF16)],
        [VMEM] * (chips + 3),
        [
            pltpu.VMEM((2 * kept, ROWS, WIDTH), BF16),
            pltpu.VMEM((3, 2 * kept, ROWS, WIDTH), F32),
        ],
    )(table, *queries, keys, values)
    near_blocks, *to_sibling = lax.optimization_barrier((near_blocks, *to_sibling))
    from_sibling = [other_core(x) for x in to_sibling]
    joined = call(join_kernel, "join", shape((3,) + wide, F32), [VMEM] * 4)(
        mine, own, *from_sibling
    )
    block_arrays = [both_blocks]
    for x in far_blocks:
        x = lax.optimization_barrier((x, joined))[0]
        block_arrays += [x, other_core(x)]
    block_arrays += [near_blocks, other_core(near_blocks)]

    messages = call(
        functools.partial(prompts_kernel, chips, each, shifts, 2 * pieces),
        "prompts",
        [shape((each, MESSAGE, WIDTH), F32)] * chips,
        [VMEM] * (4 + shifts),
    )(table, kept_queries, joined, *block_arrays)
    arrived = [messages[0]] + [other_chip(messages[s], s) for s in range(1, chips)]

    out = call(
        functools.partial(combine_kernel, chips),
        "combine",
        shape(verified_queries.shape, BF16),
        [VMEM] * chips,
    )(*arrived)
    return jnp.transpose(out, (0, 2, 1, 3))


def solution(mesh):
    placed = (
        P("req", "blk", None, None),
        P("req", "blk", None, None),
        P("req", "blk", None, None),
        P("req", "blk", None, None),
        P("req", "blk", None, None),
        P("req", "blk"),
        P("req", None),
        P("req", None),
        P("req", None),
        P("req", "blk", None, None),
        P("req", "blk", None, None),
        P("req", "blk", None),
        P("req", "blk", None),
        P("req", "blk"),
    )
    return jax.shard_map(
        functools.partial(per_device, mesh.shape["blk"], mesh.shape["req"]),
        mesh=mesh,
        in_specs=placed,
        out_specs=P("req", "blk", None, None),
        check_vma=False,
    )
```

```python
import functools

import jax
import jax.numpy as jnp
from jax import lax
from jax.experimental import pallas as pl
from jax.experimental.pallas import tpu as pltpu
from jax.sharding import PartitionSpec as P

QUERY_HEADS = 16
KEY_HEADS = 4
HEAD_SIZE = 64
GROUP = QUERY_HEADS // KEY_HEADS
POSITIONS = 8
ROWS = GROUP * POSITIONS
WIDTH = KEY_HEADS * HEAD_SIZE
MESSAGE = 3 * POSITIONS

LOWEST = float(jnp.bfloat16(-1e30))
DEAD_MARK = 64.0

F32 = jnp.float32
BF16 = jnp.bfloat16
VMEM_LIMIT = 48 * 1024 * 1024


def head_of_lane(shape):
    return lax.broadcasted_iota(jnp.int32, shape, len(shape) - 1) // HEAD_SIZE


def swap_halves(x):
    pieces = [pltpu.roll(x[:, i : i + 128], HEAD_SIZE, 1) for i in range(0, x.shape[1], 128)]
    return jnp.concatenate(pieces, axis=1)


def spread_queries(q):
    lanes = head_of_lane(q.shape)
    zero = jnp.zeros_like(q)
    return jnp.concatenate([jnp.where(lanes == c, q, zero) for c in range(KEY_HEADS)], axis=0)


def fold_heads(x):
    lanes = head_of_lane((ROWS, WIDTH))
    out = jnp.broadcast_to(x[:ROWS], (ROWS, WIDTH))
    for c in range(1, KEY_HEADS):
        out = jnp.where(lanes == c, x[c * ROWS : (c + 1) * ROWS], out)
    return out


def score(q, keys):
    return lax.dot_general(
        spread_queries(q), keys, (((1,), (1,)), ((), ())), preferred_element_type=F32
    )


def weigh(weights, values):
    ones = jnp.ones((values.shape[0], 128), BF16)
    mass = jnp.dot(weights, ones, preferred_element_type=F32)
    part = jnp.dot(weights, values, preferred_element_type=F32)
    return jnp.concatenate([mass, mass], axis=1), part


def attend(q, keys, values, live):
    masked = jnp.where(live, score(q, keys), LOWEST)
    top = jnp.max(masked, axis=1, keepdims=True)
    weights = jnp.exp(masked - top).astype(BF16)
    mass, part = weigh(weights, values)
    return fold_heads(top), fold_heads(mass), fold_heads(part)


def merge(*blocks):
    top = functools.reduce(jnp.maximum, [b[0] for b in blocks])
    lifts = [jnp.exp(b[0] - top) for b in blocks]
    mass = functools.reduce(jnp.add, [a * b[1] for a, b in zip(lifts, blocks)])
    part = functools.reduce(jnp.add, [a * b[2] for a, b in zip(lifts, blocks)])
    return top, mass, part


def spot(shape):
    lane = lax.broadcasted_iota(jnp.int32, shape, 1) % HEAD_SIZE
    return lane == lax.broadcasted_iota(jnp.int32, shape, 0) % ROWS


def pack_rows(x, spare=(None, None, None)):
    sub = lax.broadcasted_iota(jnp.int32, (POSITIONS, WIDTH), 0)
    tile = lambda i: x[i * POSITIONS : (i + 1) * POSITIONS]
    a, b, c = (jnp.zeros((1, WIDTH), x.dtype) if row is None else row for row in spare)
    return jnp.concatenate(
        [
            jnp.where(sub < 5, tile(0), pltpu.roll(tile(3), 5, 0)),
            jnp.where(sub < 5, tile(1), jnp.where(sub < 7, pltpu.roll(tile(3), 2, 0), a)),
            jnp.where(sub < 5, tile(2), jnp.where(sub < 6, b, c)),
        ],
        axis=0,
    )


def unpack_rows(x):
    sub = lax.broadcasted_iota(jnp.int32, (POSITIONS, WIDTH), 0)
    last = jnp.where(sub < 3, pltpu.roll(x[0:8], 3, 0), pltpu.roll(x[8:16], 6, 0))
    return jnp.concatenate([x, last], axis=0)


def pack_message(top, mass, part):
    rounded = top.astype(BF16).astype(F32)
    lift = jnp.exp(top - rounded)
    mass, part = mass * lift, part * lift
    high = mass.astype(BF16).astype(F32)
    at = spot((ROWS, WIDTH))
    row_of = lambda x: jnp.sum(jnp.where(at, x, 0.0), axis=0, keepdims=True)
    return pack_rows(part, (row_of(rounded), row_of(high), row_of(mass - high)))


def open_messages(messages):
    at = spot((ROWS, WIDTH))
    rows = []
    for x in messages:
        for r in (15, 21, 22):
            rows.append(jnp.where(at, x[r : r + 1], 0.0).astype(BF16))
    same_head = lax.broadcasted_iota(jnp.int32, (WIDTH, WIDTH), 0) // HEAD_SIZE == (
        lax.broadcasted_iota(jnp.int32, (WIDTH, WIDTH), 1) // HEAD_SIZE
    )
    ones = jnp.where(same_head, 1.0, 0.0).astype(BF16)
    spread = jnp.dot(jnp.concatenate(rows, axis=0), ones, preferred_element_type=F32)
    out = []
    for i, x in enumerate(messages):
        get = lambda j: spread[(3 * i + j) * ROWS : (3 * i + j + 1) * ROWS]
        out.append((get(0), get(1) + get(2), unpack_rows(x)))
    return out


def start_copies(pairs, sems):
    copies = [
        pltpu.make_async_copy(source, target, sems.at[i]) for i, (source, target) in enumerate(pairs)
    ]
    for copy in copies:
        copy.start()
    return copies


def format_queries(q):
    low = lax.broadcasted_iota(jnp.int32, (POSITIONS, 128), 1) < HEAD_SIZE
    swapped = swap_halves(q)
    rows = []
    for g in range(GROUP):
        columns = []
        for c in range(0, KEY_HEADS, 2):
            halves = []
            for half in range(2):
                tile = (GROUP * (c + half) + g) // 2
                array = q if g % 2 == half else swapped
                halves.append(array[:, tile * 128 : tile * 128 + 128])
            columns.append(jnp.where(low, halves[0], halves[1]))
        rows.append(jnp.concatenate(columns, axis=1))
    return jnp.concatenate(rows, axis=0)


def across_cores(j, chips):
    if j == 0 or j == chips - 1:
        return j
    return j + 1 if j % 2 else j - 1


def place_of(request, each, chip, core, kept):
    device = lax.div(request, each)
    distance = lax.shift_right_logical(device, 1) ^ chip
    return ((device & 1) ^ core) * kept + distance * each + lax.rem(request, each)


def parcel_kernel(
    mask_hbm, keys_hbm, values_hbm, query_hbm, blocks_ref, queries_ref, mask_ref, query, pad, sems
):
    held, rows = keys_hbm.shape[:2]
    pairs = [
        (mask_hbm, mask_ref),
        (query_hbm, query),
        (keys_hbm, blocks_ref.at[:, pl.ds(0, rows)]),
        (values_hbm, blocks_ref.at[:, pl.ds(rows, rows)]),
    ]
    copies = start_copies(pairs, sems)
    pad[...] = jnp.zeros_like(pad)
    for copy in copies:
        copy.wait()
    at = lax.broadcasted_iota(jnp.int32, (16, 128), 0) + lax.broadcasted_iota(
        jnp.int32, (16, 128), 1
    )
    for i in range(held):
        keys = blocks_ref[i, :16, :128].astype(F32)
        dead = mask_ref[0, i] != 1
        blocks_ref[i, :16, :128] = jnp.where((at == 0) & dead, DEAD_MARK, keys).astype(BF16)
    count, each = query.shape[1:3]
    for n in range(count):
        pair = query[0, n].astype(F32) * HEAD_SIZE**-0.5
        for k in range(each):
            pad[k, n : n + 1] = pair[k : k + 1]
    for k in range(each):
        queries_ref[k] = pack_rows(format_queries(pad[k])).astype(BF16)


def pair_kernel(own_ref, sibling_ref, out_ref):
    half = own_ref.shape[0]
    out_ref[:half] = own_ref[...]
    out_ref[half:] = sibling_ref[...]


def gather_kernel(*refs):
    for i, ref in enumerate(refs[:-1]):
        refs[-1][i] = ref[...]


def own_kernel(chips, each, shifts, held, *refs):
    owner_hbm, length_hbm, accepted_hbm, group_hbm = refs[:4]
    near_hbm, (keys_hbm, values_hbm) = refs[4:8], refs[8:10]
    query_ref, own_out, table_out, keys_out, values_out = refs[10:15]
    owner_ref, length_ref, accepted_ref, group_ref = refs[15:19]
    owner_row, near, rows_ref, small_sems, piece_sems = refs[19:]
    pieces, rows = keys_out.shape[:2]
    kept = chips * each
    small = start_copies(
        [
            (owner_hbm, owner_ref),
            (length_hbm, length_ref),
            (accepted_hbm, accepted_ref),
            (group_hbm, group_ref),
            (owner_hbm, owner_row),
        ]
        + [(x.at[0], near.at[j]) for j, x in enumerate(near_hbm)],
        small_sems,
    )
    large = start_copies(
        [(keys_hbm.at[0, i], keys_out.at[i]) for i in range(pieces)]
        + [(values_hbm.at[0, i], values_out.at[i]) for i in range(pieces)],
        piece_sems,
    )
    me = lax.axis_index("blk")
    z = lax.axis_index("req")
    chip, core = lax.shift_right_logical(me, 1), me & 1
    rows_ref[...] = jnp.zeros_like(rows_ref)
    for copy in small:
        copy.wait()
    count = near.shape[1]
    for n in range(count):
        for j in range(4):
            pair = near[j, n].astype(F32)
            for k in range(each):
                to = (j % 2) * POSITIONS + n
                rows_ref[j // 2, k, to : to + 1] = pair[k : k + 1]

    shape = (KEY_HEADS * ROWS, 2 * POSITIONS)
    column = lax.broadcasted_iota(jnp.int32, shape, 1)
    position = lax.broadcasted_iota(jnp.int32, shape, 0) % POSITIONS
    for k in range(each):
        live = ((column < POSITIONS) & (column < accepted_ref[0, k])) | (
            (column >= POSITIONS)
            & (column < POSITIONS + count)
            & (column - POSITIONS <= position)
        )
        query = unpack_rows(query_ref[k].astype(F32)).astype(BF16)
        got = attend(query, rows_ref[0, k].astype(BF16), rows_ref[1, k].astype(BF16), live)
        for j in range(3):
            own_out[j, k] = got[j]

    owners = owner_row[...]
    slot = lax.broadcasted_iota(jnp.int32, owners.shape, 1)
    for i in range(pieces):
        index = me * pieces + i
        owner = owner_ref[0, index]
        same = jnp.where((owners == owner) & (slot < index), 1.0, 0.0)
        rank = jnp.sum(same, axis=1, keepdims=True).astype(jnp.int32)
        place = place_of(owner, each, chip, core, kept)
        table_out[i : i + 1] = jnp.full((1, 128), place, jnp.int32)
        table_out[pieces + i : pieces + i + 1] = jnp.broadcast_to(
            length_ref[0, owner] - rank * rows, (1, 128)
        )
    for i in range(kept):
        request = ((chip ^ (i // each)) * 2 + core) * each + i % each
        group = group_ref[0, request]
        shift = z ^ lax.div(group, held)
        array = jnp.where(shift < 2, shift, (shift & ~1) + ((shift ^ core) & 1))
        to = 2 * pieces + i
        table_out[to : to + 1] = jnp.full((1, 128), array * held + lax.rem(group, held), jnp.int32)
    for copy in large:
        copy.wait()


def pieces_kernel(chips, each, *refs):
    table_ref = refs[0]
    query_refs = refs[1 : 1 + chips]
    keys, values, mine_out = refs[1 + chips : 4 + chips]
    sibling_outs = refs[4 + chips : 6 + chips]
    queries_out, queries, acc = refs[6 + chips :]
    pieces, rows = keys.shape[0], keys.shape[1]
    kept = chips * each
    core = lax.axis_index("blk") & 1
    for j in range(chips):
        distance = jnp.where(core == 0, j, across_cores(j, chips))
        handed = j > 0 and j < chips - 1 and j % 2 == 0
        for side in range(2):
            start = (1 - side if handed else side) * each
            for k in range(each):
                query = unpack_rows(query_refs[j][start + k].astype(F32))
                queries[side * kept + distance * each + k] = query.astype(BF16)
    queries_out[...] = queries[:kept]
    lane = lax.broadcasted_iota(jnp.int32, (1, rows), 1)
    places = [jnp.max(table_ref[i : i + 1]) for i in range(pieces)]
    got = []
    for i in range(pieces):
        filled = table_ref[pieces + i : pieces + i + 1]
        live = lane < jnp.concatenate([filled] * (rows // 128), axis=1)
        got.append(attend(queries[places[i]], keys[i], values[i], live))
    acc[0] = jnp.full_like(acc[0], LOWEST)
    acc[1] = jnp.zeros_like(acc[1])
    acc[2] = jnp.zeros_like(acc[2])
    for i in range(pieces):
        acc[0, places[i]] = jnp.maximum(acc[0, places[i]], got[i][0])
    for i in range(pieces):
        lift = jnp.exp(got[i][0] - acc[0, places[i]])
        acc[1, places[i]] += lift * got[i][1]
        acc[2, places[i]] += lift * got[i][2]
    mine_out[...] = acc[:, :kept]
    for i in range(kept):
        half, at = divmod(i, kept // 2)
        sibling_outs[half][at] = pack_message(*[acc[j, kept + i] for j in range(3)])


def join_kernel(mine_ref, own_ref, first_ref, second_ref, out_ref):
    half, each = first_ref.shape[0], own_ref.shape[1]
    opened = open_messages([first_ref[i] for i in range(half)] + [second_ref[i] for i in range(half)])
    for i in range(2 * half):
        blocks = [[mine_ref[j, i] for j in range(3)], opened[i]]
        if i < each:
            blocks.append([own_ref[j, i] for j in range(3)])
        joined = merge(*blocks)
        for j in range(3):
            out_ref[j, i] = joined[j]


def prompts_kernel(chips, each, first_row, *refs):
    table_ref, query_ref, joined_ref = refs[:3]
    own_ref, sibling_ref, fetched_ref, swapped_ref = refs[3:7]
    out_refs = refs[7:]
    held, rows = own_ref.shape[0], own_ref.shape[1] // 2
    far = fetched_ref.shape[0] - 1
    pairs = [
        (lambda i: own_ref[i], lambda i: sibling_ref[i]),
        (lambda i: fetched_ref[far, i], lambda i: swapped_ref[far, i]),
    ]
    for p in range(0, far, 2):
        for ref in (fetched_ref, swapped_ref):
            pairs.append(tuple(lambda i, ref=ref, at=p + side: ref[at, i] for side in range(2)))
    lane = lax.broadcasted_iota(jnp.int32, (1, 2 * rows), 1)
    got = []
    for i in range(chips * each):
        at = jnp.max(table_ref[first_row + i : first_row + i + 1])
        array, slot = lax.div(at, held), lax.rem(at, held)

        def block(side):
            out = pairs[0][side](slot)
            for j in range(1, len(pairs)):
                out = jnp.where(array == j, pairs[j][side](slot), out)
            return out

        mine, other = block(0), block(1)
        marks = jnp.where(lane < rows, mine[:1, :1].astype(F32), other[:1, :1].astype(F32))
        got.append(
            attend(
                query_ref[i],
                jnp.concatenate([mine[:rows], other[:rows]], axis=0),
                jnp.concatenate([mine[rows:], other[rows:]], axis=0),
                marks < 0.5 * DEAD_MARK,
            )
        )
    for i in range(chips * each):
        merged = merge([joined_ref[j, i] for j in range(3)], got[i])
        out_refs[i // each][i % each] = pack_message(*merged)


def combine_kernel(chips, *refs):
    message_refs, out_ref = refs[:chips], refs[chips]
    count, each = out_ref.shape[1], out_ref.shape[2]
    low = lax.broadcasted_iota(jnp.int32, (POSITIONS, 128), 1) < HEAD_SIZE
    rows = []
    opened = open_messages([ref[k] for k in range(each) for ref in message_refs])
    for k in range(each):
        _, mass, part = merge(*opened[k * chips : (k + 1) * chips])
        out = part / mass
        swapped = swap_halves(out)
        columns = []
        for head in range(0, QUERY_HEADS, 2):
            c, g = head // GROUP, head % GROUP
            tile = slice((c // 2) * 128, (c // 2) * 128 + 128)
            first, second = (out, swapped) if c % 2 == 0 else (swapped, out)
            columns.append(
                jnp.where(
                    low,
                    first[g * POSITIONS : (g + 1) * POSITIONS, tile],
                    second[(g + 1) * POSITIONS : (g + 2) * POSITIONS, tile],
                )
            )
        rows.append(jnp.concatenate(columns, axis=1))
    for n in range(count):
        out_ref[0, n] = jnp.concatenate([row[n : n + 1] for row in rows], axis=0).astype(BF16)


HBM = pl.BlockSpec(memory_space=pltpu.HBM)
VMEM = pl.BlockSpec(memory_space=pltpu.VMEM)


def in_hbm(x):
    return pltpu.with_memory_space_constraint(x, pltpu.HBM)


def call(kernel, name, out_shape, in_specs, scratch=(), cost=0):
    many = isinstance(out_shape, (list, tuple))
    return pl.pallas_call(
        kernel,
        name=name,
        out_shape=out_shape,
        in_specs=in_specs,
        out_specs=[VMEM] * len(out_shape) if many else VMEM,
        scratch_shapes=list(scratch),
        cost_estimate=pl.CostEstimate(flops=0, bytes_accessed=cost, transcendentals=0),
        compiler_params=pltpu.CompilerParams(vmem_limit_bytes=VMEM_LIMIT),
    )


def per_device(
    devices,
    shifts,
    verified_queries,
    new_keys,
    verified_value_rows,
    prior_round_keys,
    prior_round_values,
    accepted,
    group_id,
    cache_len,
    slot_owner,
    piece_cache_keys,
    piece_cache_values,
    shared_prompt_keys,
    shared_prompt_values,
    prompt_mask,
):
    shape = jax.ShapeDtypeStruct
    each = verified_queries.shape[1]
    chips = devices // 2
    pieces, piece_rows = piece_cache_keys.shape[1:3]
    held, block_rows = shared_prompt_keys.shape[:2]
    kept = chips * each

    def other_core(x):
        return lax.ppermute(x, "blk", [(i, i ^ 1) for i in range(devices)])

    def other_chip(x, s):
        return lax.ppermute(x, "blk", [(i, i ^ (2 * s)) for i in range(devices)])

    def along_req(x, even, odd):
        pairs = []
        for i in range(devices * shifts):
            d, z = divmod(i, shifts)
            pairs.append((i, d * shifts + (z ^ (odd if d % 2 else even))))
        return lax.ppermute(x, ("blk", "req"), pairs)

    verified_queries, prior_round_keys, new_keys, prior_round_values, verified_value_rows = (
        jnp.transpose(x, (0, 2, 1, 3))
        for x in (
            verified_queries, prior_round_keys, new_keys, prior_round_values, verified_value_rows,
        )
    )
    near = (prior_round_keys, new_keys, prior_round_values, verified_value_rows)
    count = verified_queries.shape[1]
    block_size = 2 * block_rows
    piece_shape = (pieces, piece_rows, WIDTH)
    own_blocks, own_queries = call(
        parcel_kernel,
        "parcel",
        [
            shape((held, block_size, WIDTH), BF16),
            shape((each, MESSAGE, WIDTH), BF16),
        ],
        [HBM] * 4,
        [
            pltpu.SMEM((1, held), jnp.int32),
            pltpu.VMEM(verified_queries.shape, BF16),
            pltpu.VMEM((each, POSITIONS, QUERY_HEADS * HEAD_SIZE), F32),
            pltpu.SemaphoreType.DMA((4,)),
        ],
    )(
        *(
            in_hbm(x)
            for x in (prompt_mask.T, shared_prompt_keys, shared_prompt_values, verified_queries)
        )
    )
    sibling_blocks, sibling_queries, later_blocks = lax.optimization_barrier(
        (other_core(own_blocks), other_core(own_queries), own_blocks)
    )
    fetched = []
    for s in range(2, shifts, 2):
        fetched += [along_req(x, s, s + 1) for x in (own_blocks, sibling_blocks)]
    fetched.append(along_req(later_blocks, 1, 1))
    chip_queries = call(
        pair_kernel, "pair", shape((2 * each, MESSAGE, WIDTH), BF16), [VMEM] * 2
    )(own_queries, sibling_queries)

    own, table, keys, values = call(
        functools.partial(own_kernel, chips, each, shifts, held),
        "own",
        [
            shape((3, each, ROWS, WIDTH), F32),
            shape((2 * pieces + kept, 128), jnp.int32),
            shape(piece_shape, BF16),
            shape(piece_shape, BF16),
        ],
        [HBM] * 10 + [VMEM],
        [
            pltpu.SMEM(slot_owner.shape, jnp.int32),
            pltpu.SMEM(cache_len.shape, jnp.int32),
            pltpu.SMEM(accepted.shape, jnp.int32),
            pltpu.SMEM(group_id.shape, jnp.int32),
            pltpu.VMEM(slot_owner.shape, jnp.int32),
            pltpu.VMEM((4, count, each, WIDTH), BF16),
            pltpu.VMEM((2, each, 2 * POSITIONS, WIDTH), F32),
            pltpu.SemaphoreType.DMA((9,)),
            pltpu.SemaphoreType.DMA((2 * pieces,)),
        ],
        8 * 1024 * 1024,
    )(
        *(
            in_hbm(x)
            for x in (slot_owner, cache_len, accepted, group_id)
            + near
            + (piece_cache_keys, piece_cache_values)
        ),
        chip_queries,
    )

    queries = [chip_queries]
    for s in range(1, chips - 1, 2):
        taken = lax.ppermute(
            chip_queries,
            "blk",
            [(i, i ^ (2 * (across_cores(s, chips) if i % 2 else s))) for i in range(devices)],
        )
        taken = lax.optimization_barrier((taken, table))[0]
        queries += [taken, other_core(taken)]
    if chips > 1:
        queries.append(other_chip(chip_queries, chips - 1))

    wide = (kept, ROWS, WIDTH)
    mine, *to_sibling, kept_queries = call(
        functools.partial(pieces_kernel, chips, each),
        "pieces",
        [shape((3,) + wide, F32)]
        + [shape((kept // 2, MESSAGE, WIDTH), F32)] * 2
        + [shape(wide, BF16)],
        [VMEM] * (chips + 3),
        [
            pltpu.VMEM((2 * kept, ROWS, WIDTH), BF16),
            pltpu.VMEM((3, 2 * kept, ROWS, WIDTH), F32),
        ],
    )(table, *queries, keys, values)
    from_sibling = [other_core(x) for x in to_sibling]
    joined = call(join_kernel, "join", shape((3,) + wide, F32), [VMEM] * 4)(
        mine, own, *from_sibling
    )
    fetched = lax.optimization_barrier((kept_queries, *fetched))[1:]
    gathered = call(
        gather_kernel,
        "gather",
        shape((len(fetched), held, block_size, WIDTH), BF16),
        [VMEM] * len(fetched),
    )(*fetched)

    messages = call(
        functools.partial(prompts_kernel, chips, each, 2 * pieces),
        "prompts",
        [shape((each, MESSAGE, WIDTH), F32)] * chips,
        [VMEM] * 7,
    )(table, kept_queries, joined, own_blocks, sibling_blocks, gathered, other_core(gathered))
    arrived = [messages[0]] + [other_chip(messages[s], s) for s in range(1, chips)]

    out = call(
        functools.partial(combine_kernel, chips),
        "combine",
        shape(verified_queries.shape, BF16),
        [VMEM] * chips,
    )(*arrived)
    return jnp.transpose(out, (0, 2, 1, 3))


def solution(mesh):
    placed = (
        P("req", "blk", None, None),
        P("req", "blk", None, None),
        P("req", "blk", None, None),
        P("req", "blk", None, None),
        P("req", "blk", None, None),
        P("req", "blk"),
        P("req", None),
        P("req", None),
        P("req", None),
        P("req", "blk", None, None),
        P("req", "blk", None, None),
        P("req", "blk", None),
        P("req", "blk", None),
        P("req", "blk"),
    )
    return jax.shard_map(
        functools.partial(per_device, mesh.shape["blk"], mesh.shape["req"]),
        mesh=mesh,
        in_specs=placed,
        out_specs=P("req", "blk", None, None),
        check_vma=False,
    )
```

```python
import functools

import jax
import jax.numpy as jnp
from jax import lax
from jax.experimental import pallas as pl
from jax.experimental.pallas import tpu as pltpu
from jax.sharding import PartitionSpec as P

QUERY_HEADS = 16
KEY_HEADS = 4
HEAD_SIZE = 64
GROUP = QUERY_HEADS // KEY_HEADS
POSITIONS = 8
ROWS = GROUP * POSITIONS
WIDTH = KEY_HEADS * HEAD_SIZE
MESSAGE = 3 * POSITIONS

LOWEST = float(jnp.bfloat16(-1e30))
DEAD_MARK = 64.0

F32 = jnp.float32
BF16 = jnp.bfloat16
VMEM_LIMIT = 48 * 1024 * 1024


def head_of_lane(shape):
    return lax.broadcasted_iota(jnp.int32, shape, len(shape) - 1) // HEAD_SIZE


def swap_halves(x):
    pieces = [pltpu.roll(x[:, i : i + 128], HEAD_SIZE, 1) for i in range(0, x.shape[1], 128)]
    return jnp.concatenate(pieces, axis=1)


def spread_queries(q):
    lanes = head_of_lane(q.shape)
    zero = jnp.zeros_like(q)
    return jnp.concatenate([jnp.where(lanes == c, q, zero) for c in range(KEY_HEADS)], axis=0)


def fold_heads(x):
    lanes = head_of_lane((ROWS, WIDTH))
    out = jnp.broadcast_to(x[:ROWS], (ROWS, WIDTH))
    for c in range(1, KEY_HEADS):
        out = jnp.where(lanes == c, x[c * ROWS : (c + 1) * ROWS], out)
    return out


def score(q, keys):
    return lax.dot_general(
        spread_queries(q), keys, (((1,), (1,)), ((), ())), preferred_element_type=F32
    )


def attend(q, keys, values, live, wide):
    masked = jnp.where(live, score(q, keys), LOWEST)
    top = jnp.max(masked, axis=1, keepdims=True)
    weights = jnp.exp(masked - top).astype(BF16)
    if wide:
        values = jnp.concatenate([values, jnp.ones((values.shape[0], 128), BF16)], axis=1)
    part = jnp.dot(weights, values, preferred_element_type=F32)
    if wide:
        mass = jnp.concatenate([part[:, WIDTH:]] * 2, axis=1)
    else:
        mass = jnp.sum(weights.astype(F32), axis=1, keepdims=True)
    return fold_heads(top), fold_heads(mass), fold_heads(part[:, :WIDTH])


def merge(*blocks):
    top = functools.reduce(jnp.maximum, [b[0] for b in blocks])
    lifts = [jnp.exp(b[0] - top) for b in blocks]
    mass = functools.reduce(jnp.add, [a * b[1] for a, b in zip(lifts, blocks)])
    part = functools.reduce(jnp.add, [a * b[2] for a, b in zip(lifts, blocks)])
    return top, mass, part


def spot(shape):
    lane = lax.broadcasted_iota(jnp.int32, shape, 1) % HEAD_SIZE
    return lane == lax.broadcasted_iota(jnp.int32, shape, 0) % ROWS


def pack_rows(x, spare=(None, None, None)):
    sub = lax.broadcasted_iota(jnp.int32, (POSITIONS, WIDTH), 0)
    tile = lambda i: x[i * POSITIONS : (i + 1) * POSITIONS]
    a, b, c = (jnp.zeros((1, WIDTH), x.dtype) if row is None else row for row in spare)
    return jnp.concatenate(
        [
            jnp.where(sub < 5, tile(0), pltpu.roll(tile(3), 5, 0)),
            jnp.where(sub < 5, tile(1), jnp.where(sub < 7, pltpu.roll(tile(3), 2, 0), a)),
            jnp.where(sub < 5, tile(2), jnp.where(sub < 6, b, c)),
        ],
        axis=0,
    )


def unpack_rows(x):
    sub = lax.broadcasted_iota(jnp.int32, (POSITIONS, WIDTH), 0)
    last = jnp.where(sub < 3, pltpu.roll(x[0:8], 3, 0), pltpu.roll(x[8:16], 6, 0))
    return jnp.concatenate([x, last], axis=0)


def pack_message(top, mass, part):
    rounded = top.astype(BF16).astype(F32)
    lift = jnp.exp(top - rounded)
    mass, part = mass * lift, part * lift
    high = mass.astype(BF16).astype(F32)
    at = spot((ROWS, WIDTH))
    row_of = lambda x: jnp.sum(jnp.where(at, x, 0.0), axis=0, keepdims=True)
    return pack_rows(part, (row_of(rounded), row_of(high), row_of(mass - high)))


def open_messages(messages):
    at = spot((ROWS, WIDTH))
    rows = []
    for x in messages:
        for r in (15, 21, 22):
            rows.append(jnp.where(at, x[r : r + 1], 0.0).astype(BF16))
    same_head = lax.broadcasted_iota(jnp.int32, (WIDTH, WIDTH), 0) // HEAD_SIZE == (
        lax.broadcasted_iota(jnp.int32, (WIDTH, WIDTH), 1) // HEAD_SIZE
    )
    ones = jnp.where(same_head, 1.0, 0.0).astype(BF16)
    spread = jnp.dot(jnp.concatenate(rows, axis=0), ones, preferred_element_type=F32)
    out = []
    for i, x in enumerate(messages):
        get = lambda j: spread[(3 * i + j) * ROWS : (3 * i + j + 1) * ROWS]
        out.append((get(0), get(1) + get(2), unpack_rows(x)))
    return out


def start_copies(pairs, sems):
    copies = [
        pltpu.make_async_copy(source, target, sems.at[i]) for i, (source, target) in enumerate(pairs)
    ]
    for copy in copies:
        copy.start()
    return copies


def format_queries(q):
    low = lax.broadcasted_iota(jnp.int32, (POSITIONS, 128), 1) < HEAD_SIZE
    swapped = swap_halves(q)
    rows = []
    for g in range(GROUP):
        columns = []
        for c in range(0, KEY_HEADS, 2):
            halves = []
            for half in range(2):
                tile = (GROUP * (c + half) + g) // 2
                array = q if g % 2 == half else swapped
                halves.append(array[:, tile * 128 : tile * 128 + 128])
            columns.append(jnp.where(low, halves[0], halves[1]))
        rows.append(jnp.concatenate(columns, axis=1))
    return jnp.concatenate(rows, axis=0)


def across_cores(j, chips):
    if j == 0 or j == chips - 1:
        return j
    return j + 1 if j % 2 else j - 1


def place_of(request, each, chip, core, kept):
    device = lax.div(request, each)
    distance = lax.shift_right_logical(device, 1) ^ chip
    return ((device & 1) ^ core) * kept + distance * each + lax.rem(request, each)


def parcel_kernel(
    mask_hbm, keys_hbm, values_hbm, query_hbm, blocks_ref, queries_ref, mask_ref, query, pad, sems
):
    held, rows = keys_hbm.shape[:2]
    pairs = [
        (mask_hbm, mask_ref),
        (query_hbm, query),
        (keys_hbm, blocks_ref.at[:, pl.ds(0, rows)]),
        (values_hbm, blocks_ref.at[:, pl.ds(rows, rows)]),
    ]
    copies = start_copies(pairs, sems)
    pad[...] = jnp.zeros_like(pad)
    for copy in copies:
        copy.wait()
    at = lax.broadcasted_iota(jnp.int32, (16, 128), 0) + lax.broadcasted_iota(
        jnp.int32, (16, 128), 1
    )
    for i in range(held):
        keys = blocks_ref[i, :16, :128].astype(F32)
        dead = mask_ref[0, i] != 1
        blocks_ref[i, :16, :128] = jnp.where((at == 0) & dead, DEAD_MARK, keys).astype(BF16)
    count, each = query.shape[1:3]
    for n in range(count):
        pair = query[0, n].astype(F32) * HEAD_SIZE**-0.5
        for k in range(each):
            pad[k, n : n + 1] = pair[k : k + 1]
    for k in range(each):
        queries_ref[k] = pack_rows(format_queries(pad[k])).astype(BF16)


def pair_kernel(own_ref, sibling_ref, out_ref):
    half = own_ref.shape[0]
    out_ref[:half] = own_ref[...]
    out_ref[half:] = sibling_ref[...]


def gather_kernel(*refs):
    for i, ref in enumerate(refs[:-1]):
        refs[-1][i] = ref[...]


def own_kernel(chips, each, shifts, held, *refs):
    owner_hbm, length_hbm, accepted_hbm, group_hbm = refs[:4]
    near_hbm, (keys_hbm, values_hbm) = refs[4:8], refs[8:10]
    query_ref, own_out, table_out, keys_out, values_out = refs[10:15]
    owner_ref, length_ref, accepted_ref, group_ref = refs[15:19]
    owner_row, near, rows_ref, small_sems, piece_sems = refs[19:]
    pieces, rows = keys_out.shape[:2]
    kept = chips * each
    small = start_copies(
        [
            (owner_hbm, owner_ref),
            (length_hbm, length_ref),
            (accepted_hbm, accepted_ref),
            (group_hbm, group_ref),
            (owner_hbm, owner_row),
        ]
        + [(x.at[0], near.at[j]) for j, x in enumerate(near_hbm)],
        small_sems,
    )
    large = start_copies(
        [(keys_hbm.at[0, i], keys_out.at[i]) for i in range(pieces)]
        + [(values_hbm.at[0, i], values_out.at[i]) for i in range(pieces)],
        piece_sems,
    )
    me = lax.axis_index("blk")
    z = lax.axis_index("req")
    chip, core = lax.shift_right_logical(me, 1), me & 1
    rows_ref[...] = jnp.zeros_like(rows_ref)
    for copy in small:
        copy.wait()
    count = near.shape[1]
    for n in range(count):
        for j in range(4):
            pair = near[j, n].astype(F32)
            for k in range(each):
                to = (j % 2) * POSITIONS + n
                rows_ref[j // 2, k, to : to + 1] = pair[k : k + 1]

    shape = (KEY_HEADS * ROWS, 2 * POSITIONS)
    column = lax.broadcasted_iota(jnp.int32, shape, 1)
    position = lax.broadcasted_iota(jnp.int32, shape, 0) % POSITIONS
    for k in range(each):
        live = ((column < POSITIONS) & (column < accepted_ref[0, k])) | (
            (column >= POSITIONS)
            & (column < POSITIONS + count)
            & (column - POSITIONS <= position)
        )
        query = unpack_rows(query_ref[k].astype(F32)).astype(BF16)
        got = attend(query, rows_ref[0, k].astype(BF16), rows_ref[1, k].astype(BF16), live, False)
        for j in range(3):
            own_out[j, k] = got[j]

    owners = owner_row[...]
    slot = lax.broadcasted_iota(jnp.int32, owners.shape, 1)
    for i in range(pieces):
        index = me * pieces + i
        owner = owner_ref[0, index]
        same = jnp.where((owners == owner) & (slot < index), 1.0, 0.0)
        rank = jnp.sum(same, axis=1, keepdims=True).astype(jnp.int32)
        place = place_of(owner, each, chip, core, kept)
        table_out[i : i + 1] = jnp.full((1, 128), place, jnp.int32)
        table_out[pieces + i : pieces + i + 1] = jnp.broadcast_to(
            length_ref[0, owner] - rank * rows, (1, 128)
        )
    for i in range(kept):
        request = ((chip ^ (i // each)) * 2 + core) * each + i % each
        group = group_ref[0, request]
        shift = z ^ lax.div(group, held)
        array = jnp.where(shift < 2, shift, (shift & ~1) + ((shift ^ core) & 1))
        to = 2 * pieces + i
        table_out[to : to + 1] = jnp.full((1, 128), array * held + lax.rem(group, held), jnp.int32)
    for copy in large:
        copy.wait()


def pieces_kernel(chips, each, *refs):
    table_ref = refs[0]
    query_refs = refs[1 : 1 + chips]
    keys, values, mine_out = refs[1 + chips : 4 + chips]
    sibling_outs = refs[4 + chips : 6 + chips]
    queries_out, queries, acc = refs[6 + chips :]
    pieces, rows = keys.shape[0], keys.shape[1]
    kept = chips * each
    core = lax.axis_index("blk") & 1
    for j in range(chips):
        distance = jnp.where(core == 0, j, across_cores(j, chips))
        handed = j > 0 and j < chips - 1 and j % 2 == 0
        for side in range(2):
            start = (1 - side if handed else side) * each
            for k in range(each):
                query = unpack_rows(query_refs[j][start + k].astype(F32))
                queries[side * kept + distance * each + k] = query.astype(BF16)
    queries_out[...] = queries[:kept]
    lane = lax.broadcasted_iota(jnp.int32, (1, rows), 1)
    places = [jnp.max(table_ref[i : i + 1]) for i in range(pieces)]
    got = []
    for i in range(pieces):
        filled = table_ref[pieces + i : pieces + i + 1]
        live = lane < jnp.concatenate([filled] * (rows // 128), axis=1)
        got.append(attend(queries[places[i]], keys[i], values[i], live, True))
    acc[0] = jnp.full_like(acc[0], LOWEST)
    acc[1] = jnp.zeros_like(acc[1])
    acc[2] = jnp.zeros_like(acc[2])
    for i in range(pieces):
        acc[0, places[i]] = jnp.maximum(acc[0, places[i]], got[i][0])
    for i in range(pieces):
        lift = jnp.exp(got[i][0] - acc[0, places[i]])
        acc[1, places[i]] += lift * got[i][1]
        acc[2, places[i]] += lift * got[i][2]
    mine_out[...] = acc[:, :kept]
    for i in range(kept):
        half, at = divmod(i, kept // 2)
        sibling_outs[half][at] = pack_message(*[acc[j, kept + i] for j in range(3)])


def join_kernel(mine_ref, own_ref, first_ref, second_ref, out_ref):
    half, each = first_ref.shape[0], own_ref.shape[1]
    opened = open_messages([first_ref[i] for i in range(half)] + [second_ref[i] for i in range(half)])
    for i in range(2 * half):
        blocks = [[mine_ref[j, i] for j in range(3)], opened[i]]
        if i < each:
            blocks.append([own_ref[j, i] for j in range(3)])
        joined = merge(*blocks)
        for j in range(3):
            out_ref[j, i] = joined[j]


def prompts_kernel(chips, each, first_row, *refs):
    table_ref, query_ref, joined_ref = refs[:3]
    own_ref, sibling_ref, fetched_ref, swapped_ref = refs[3:7]
    out_refs = refs[7:]
    held, rows = own_ref.shape[0], own_ref.shape[1] // 2
    far = fetched_ref.shape[0] - 1
    pairs = [
        (lambda i: own_ref[i], lambda i: sibling_ref[i]),
        (lambda i: fetched_ref[far, i], lambda i: swapped_ref[far, i]),
    ]
    for p in range(0, far, 2):
        for ref in (fetched_ref, swapped_ref):
            pairs.append(tuple(lambda i, ref=ref, at=p + side: ref[at, i] for side in range(2)))
    lane = lax.broadcasted_iota(jnp.int32, (1, 2 * rows), 1)
    got = []
    for i in range(chips * each):
        at = jnp.max(table_ref[first_row + i : first_row + i + 1])
        array, slot = lax.div(at, held), lax.rem(at, held)

        def block(side):
            out = pairs[0][side](slot)
            for j in range(1, len(pairs)):
                out = jnp.where(array == j, pairs[j][side](slot), out)
            return out

        mine, other = block(0), block(1)
        marks = jnp.where(lane < rows, mine[:1, :1].astype(F32), other[:1, :1].astype(F32))
        got.append(
            attend(
                query_ref[i],
                jnp.concatenate([mine[:rows], other[:rows]], axis=0),
                jnp.concatenate([mine[rows:], other[rows:]], axis=0),
                marks < 0.5 * DEAD_MARK,
                False,
            )
        )
    for i in range(chips * each):
        merged = merge([joined_ref[j, i] for j in range(3)], got[i])
        out_refs[i // each][i % each] = pack_message(*merged)


def combine_kernel(chips, *refs):
    message_refs, out_ref = refs[:chips], refs[chips]
    count, each = out_ref.shape[1], out_ref.shape[2]
    low = lax.broadcasted_iota(jnp.int32, (POSITIONS, 128), 1) < HEAD_SIZE
    rows = []
    opened = open_messages([ref[k] for k in range(each) for ref in message_refs])
    for k in range(each):
        _, mass, part = merge(*opened[k * chips : (k + 1) * chips])
        out = part / mass
        swapped = swap_halves(out)
        columns = []
        for head in range(0, QUERY_HEADS, 2):
            c, g = head // GROUP, head % GROUP
            tile = slice((c // 2) * 128, (c // 2) * 128 + 128)
            first, second = (out, swapped) if c % 2 == 0 else (swapped, out)
            columns.append(
                jnp.where(
                    low,
                    first[g * POSITIONS : (g + 1) * POSITIONS, tile],
                    second[(g + 1) * POSITIONS : (g + 2) * POSITIONS, tile],
                )
            )
        rows.append(jnp.concatenate(columns, axis=1))
    for n in range(count):
        out_ref[0, n] = jnp.concatenate([row[n : n + 1] for row in rows], axis=0).astype(BF16)


HBM = pl.BlockSpec(memory_space=pltpu.HBM)
VMEM = pl.BlockSpec(memory_space=pltpu.VMEM)


def in_hbm(x):
    return pltpu.with_memory_space_constraint(x, pltpu.HBM)


def call(kernel, name, out_shape, in_specs, scratch=(), cost=0):
    many = isinstance(out_shape, (list, tuple))
    return pl.pallas_call(
        kernel,
        name=name,
        out_shape=out_shape,
        in_specs=in_specs,
        out_specs=[VMEM] * len(out_shape) if many else VMEM,
        scratch_shapes=list(scratch),
        cost_estimate=pl.CostEstimate(flops=0, bytes_accessed=cost, transcendentals=0),
        compiler_params=pltpu.CompilerParams(vmem_limit_bytes=VMEM_LIMIT),
    )


def per_device(
    devices,
    shifts,
    verified_queries,
    new_keys,
    verified_value_rows,
    prior_round_keys,
    prior_round_values,
    accepted,
    group_id,
    cache_len,
    slot_owner,
    piece_cache_keys,
    piece_cache_values,
    shared_prompt_keys,
    shared_prompt_values,
    prompt_mask,
):
    shape = jax.ShapeDtypeStruct
    each = verified_queries.shape[1]
    chips = devices // 2
    pieces, piece_rows = piece_cache_keys.shape[1:3]
    held, block_rows = shared_prompt_keys.shape[:2]
    kept = chips * each

    def other_core(x):
        return lax.ppermute(x, "blk", [(i, i ^ 1) for i in range(devices)])

    def other_chip(x, s):
        return lax.ppermute(x, "blk", [(i, i ^ (2 * s)) for i in range(devices)])

    def along_req(x, even, odd):
        pairs = []
        for i in range(devices * shifts):
            d, z = divmod(i, shifts)
            pairs.append((i, d * shifts + (z ^ (odd if d % 2 else even))))
        return lax.ppermute(x, ("blk", "req"), pairs)

    verified_queries, prior_round_keys, new_keys, prior_round_values, verified_value_rows = (
        jnp.transpose(x, (0, 2, 1, 3))
        for x in (
            verified_queries, prior_round_keys, new_keys, prior_round_values, verified_value_rows,
        )
    )
    near = (prior_round_keys, new_keys, prior_round_values, verified_value_rows)
    count = verified_queries.shape[1]
    block_size = 2 * block_rows
    piece_shape = (pieces, piece_rows, WIDTH)
    own_blocks, own_queries = call(
        parcel_kernel,
        "parcel",
        [
            shape((held, block_size, WIDTH), BF16),
            shape((each, MESSAGE, WIDTH), BF16),
        ],
        [HBM] * 4,
        [
            pltpu.SMEM((1, held), jnp.int32),
            pltpu.VMEM(verified_queries.shape, BF16),
            pltpu.VMEM((each, POSITIONS, QUERY_HEADS * HEAD_SIZE), F32),
            pltpu.SemaphoreType.DMA((4,)),
        ],
    )(
        *(
            in_hbm(x)
            for x in (prompt_mask.T, shared_prompt_keys, shared_prompt_values, verified_queries)
        )
    )
    sibling_blocks, sibling_queries, later_blocks = lax.optimization_barrier(
        (other_core(own_blocks), other_core(own_queries), own_blocks)
    )
    fetched = []
    for s in range(2, shifts, 2):
        fetched += [along_req(x, s, s + 1) for x in (own_blocks, sibling_blocks)]
    fetched.append(along_req(later_blocks, 1, 1))
    chip_queries = call(
        pair_kernel, "pair", shape((2 * each, MESSAGE, WIDTH), BF16), [VMEM] * 2
    )(own_queries, sibling_queries)

    own, table, keys, values = call(
        functools.partial(own_kernel, chips, each, shifts, held),
        "own",
        [
            shape((3, each, ROWS, WIDTH), F32),
            shape((2 * pieces + kept, 128), jnp.int32),
            shape(piece_shape, BF16),
            shape(piece_shape, BF16),
        ],
        [HBM] * 10 + [VMEM],
        [
            pltpu.SMEM(slot_owner.shape, jnp.int32),
            pltpu.SMEM(cache_len.shape, jnp.int32),
            pltpu.SMEM(accepted.shape, jnp.int32),
            pltpu.SMEM(group_id.shape, jnp.int32),
            pltpu.VMEM(slot_owner.shape, jnp.int32),
            pltpu.VMEM((4, count, each, WIDTH), BF16),
            pltpu.VMEM((2, each, 2 * POSITIONS, WIDTH), F32),
            pltpu.SemaphoreType.DMA((9,)),
            pltpu.SemaphoreType.DMA((2 * pieces,)),
        ],
        8 * 1024 * 1024,
    )(
        *(
            in_hbm(x)
            for x in (slot_owner, cache_len, accepted, group_id)
            + near
            + (piece_cache_keys, piece_cache_values)
        ),
        chip_queries,
    )

    queries = [chip_queries]
    for s in range(1, chips - 1, 2):
        taken = lax.ppermute(
            chip_queries,
            "blk",
            [(i, i ^ (2 * (across_cores(s, chips) if i % 2 else s))) for i in range(devices)],
        )
        taken = lax.optimization_barrier((taken, table))[0]
        queries += [taken, other_core(taken)]
    if chips > 1:
        queries.append(other_chip(chip_queries, chips - 1))

    wide = (kept, ROWS, WIDTH)
    mine, *to_sibling, kept_queries = call(
        functools.partial(pieces_kernel, chips, each),
        "pieces",
        [shape((3,) + wide, F32)]
        + [shape((kept // 2, MESSAGE, WIDTH), F32)] * 2
        + [shape(wide, BF16)],
        [VMEM] * (chips + 3),
        [
            pltpu.VMEM((2 * kept, ROWS, WIDTH), BF16),
            pltpu.VMEM((3, 2 * kept, ROWS, WIDTH), F32),
        ],
    )(table, *queries, keys, values)
    from_sibling = [other_core(x) for x in to_sibling]
    joined = call(join_kernel, "join", shape((3,) + wide, F32), [VMEM] * 4)(
        mine, own, *from_sibling
    )
    fetched = lax.optimization_barrier((kept_queries, *fetched))[1:]
    gathered = call(
        gather_kernel,
        "gather",
        shape((len(fetched), held, block_size, WIDTH), BF16),
        [VMEM] * len(fetched),
    )(*fetched)

    messages = call(
        functools.partial(prompts_kernel, chips, each, 2 * pieces),
        "prompts",
        [shape((each, MESSAGE, WIDTH), F32)] * chips,
        [VMEM] * 7,
    )(table, kept_queries, joined, own_blocks, sibling_blocks, gathered, other_core(gathered))
    arrived = [messages[0]] + [other_chip(messages[s], s) for s in range(chips - 1, 0, -1)]

    out = call(
        functools.partial(combine_kernel, chips),
        "combine",
        shape(verified_queries.shape, BF16),
        [VMEM] * chips,
    )(*arrived)
    return jnp.transpose(out, (0, 2, 1, 3))


def solution(mesh):
    placed = (
        P("req", "blk", None, None),
        P("req", "blk", None, None),
        P("req", "blk", None, None),
        P("req", "blk", None, None),
        P("req", "blk", None, None),
        P("req", "blk"),
        P("req", None),
        P("req", None),
        P("req", None),
        P("req", "blk", None, None),
        P("req", "blk", None, None),
        P("req", "blk", None),
        P("req", "blk", None),
        P("req", "blk"),
    )
    return jax.shard_map(
        functools.partial(per_device, mesh.shape["blk"], mesh.shape["req"]),
        mesh=mesh,
        in_specs=placed,
        out_specs=P("req", "blk", None, None),
        check_vma=False,
    )
```

```python
import functools

import jax
import jax.numpy as jnp
from jax import lax
from jax.experimental import pallas as pl
from jax.experimental.pallas import tpu as pltpu
from jax.sharding import PartitionSpec as P

QUERY_HEADS = 16
KEY_HEADS = 4
HEAD_SIZE = 64
GROUP = QUERY_HEADS // KEY_HEADS
POSITIONS = 8
ROWS = GROUP * POSITIONS
WIDTH = KEY_HEADS * HEAD_SIZE
MESSAGE = 3 * POSITIONS

LOWEST = float(jnp.bfloat16(-1e30))
DEAD_MARK = 64.0

F32 = jnp.float32
BF16 = jnp.bfloat16
VMEM_LIMIT = 48 * 1024 * 1024


def head_of_lane(shape):
    return lax.broadcasted_iota(jnp.int32, shape, len(shape) - 1) // HEAD_SIZE


def swap_halves(x):
    pieces = [pltpu.roll(x[:, i : i + 128], HEAD_SIZE, 1) for i in range(0, x.shape[1], 128)]
    return jnp.concatenate(pieces, axis=1)


def spread_queries(q):
    lanes = head_of_lane(q.shape)
    zero = jnp.zeros_like(q)
    return jnp.concatenate([jnp.where(lanes == c, q, zero) for c in range(KEY_HEADS)], axis=0)


def fold_heads(x):
    lanes = head_of_lane((ROWS, WIDTH))
    out = jnp.broadcast_to(x[:ROWS], (ROWS, WIDTH))
    for c in range(1, KEY_HEADS):
        out = jnp.where(lanes == c, x[c * ROWS : (c + 1) * ROWS], out)
    return out


def score(q, keys):
    return lax.dot_general(
        spread_queries(q), keys, (((1,), (1,)), ((), ())), preferred_element_type=F32
    )


def attend(q, keys, values, live, wide):
    masked = jnp.where(live, score(q, keys), LOWEST)
    top = jnp.max(masked, axis=1, keepdims=True)
    weights = jnp.exp(masked - top).astype(BF16)
    if wide:
        values = jnp.concatenate([values, jnp.ones((values.shape[0], 128), BF16)], axis=1)
    part = jnp.dot(weights, values, preferred_element_type=F32)
    if wide:
        mass = jnp.concatenate([part[:, WIDTH:]] * 2, axis=1)
    else:
        mass = jnp.sum(weights.astype(F32), axis=1, keepdims=True)
    return fold_heads(top), fold_heads(mass), fold_heads(part[:, :WIDTH])


def merge(*blocks):
    top = functools.reduce(jnp.maximum, [b[0] for b in blocks])
    lifts = [jnp.exp(b[0] - top) for b in blocks]
    mass = functools.reduce(jnp.add, [a * b[1] for a, b in zip(lifts, blocks)])
    part = functools.reduce(jnp.add, [a * b[2] for a, b in zip(lifts, blocks)])
    return top, mass, part


def spot(shape):
    lane = lax.broadcasted_iota(jnp.int32, shape, 1) % HEAD_SIZE
    return lane == lax.broadcasted_iota(jnp.int32, shape, 0) % ROWS


def pack_rows(x, spare=(None, None, None)):
    sub = lax.broadcasted_iota(jnp.int32, (POSITIONS, WIDTH), 0)
    tile = lambda i: x[i * POSITIONS : (i + 1) * POSITIONS]
    a, b, c = (jnp.zeros((1, WIDTH), x.dtype) if row is None else row for row in spare)
    return jnp.concatenate(
        [
            jnp.where(sub < 5, tile(0), pltpu.roll(tile(3), 5, 0)),
            jnp.where(sub < 5, tile(1), jnp.where(sub < 7, pltpu.roll(tile(3), 2, 0), a)),
            jnp.where(sub < 5, tile(2), jnp.where(sub < 6, b, c)),
        ],
        axis=0,
    )


def unpack_rows(x):
    sub = lax.broadcasted_iota(jnp.int32, (POSITIONS, WIDTH), 0)
    last = jnp.where(sub < 3, pltpu.roll(x[0:8], 3, 0), pltpu.roll(x[8:16], 6, 0))
    return jnp.concatenate([x, last], axis=0)


def pack_message(top, mass, part):
    rounded = top.astype(BF16).astype(F32)
    lift = jnp.exp(top - rounded)
    mass, part = mass * lift, part * lift
    high = mass.astype(BF16).astype(F32)
    at = spot((ROWS, WIDTH))
    row_of = lambda x: jnp.sum(jnp.where(at, x, 0.0), axis=0, keepdims=True)
    return pack_rows(part, (row_of(rounded), row_of(high), row_of(mass - high)))


def open_messages(messages):
    at = spot((ROWS, WIDTH))
    rows = []
    for x in messages:
        for r in (15, 21, 22):
            rows.append(jnp.where(at, x[r : r + 1], 0.0).astype(BF16))
    same_head = lax.broadcasted_iota(jnp.int32, (WIDTH, WIDTH), 0) // HEAD_SIZE == (
        lax.broadcasted_iota(jnp.int32, (WIDTH, WIDTH), 1) // HEAD_SIZE
    )
    ones = jnp.where(same_head, 1.0, 0.0).astype(BF16)
    spread = jnp.dot(jnp.concatenate(rows, axis=0), ones, preferred_element_type=F32)
    out = []
    for i, x in enumerate(messages):
        get = lambda j: spread[(3 * i + j) * ROWS : (3 * i + j + 1) * ROWS]
        out.append((get(0), get(1) + get(2), unpack_rows(x)))
    return out


def start_copies(pairs, sems):
    copies = [
        pltpu.make_async_copy(source, target, sems.at[i]) for i, (source, target) in enumerate(pairs)
    ]
    for copy in copies:
        copy.start()
    return copies


def format_queries(q):
    low = lax.broadcasted_iota(jnp.int32, (POSITIONS, 128), 1) < HEAD_SIZE
    swapped = swap_halves(q)
    rows = []
    for g in range(GROUP):
        columns = []
        for c in range(0, KEY_HEADS, 2):
            halves = []
            for half in range(2):
                tile = (GROUP * (c + half) + g) // 2
                array = q if g % 2 == half else swapped
                halves.append(array[:, tile * 128 : tile * 128 + 128])
            columns.append(jnp.where(low, halves[0], halves[1]))
        rows.append(jnp.concatenate(columns, axis=1))
    return jnp.concatenate(rows, axis=0)


def across_cores(j, chips):
    if j == 0 or j == chips - 1:
        return j
    return j + 1 if j % 2 else j - 1


def place_of(request, each, chip, core, kept):
    device = lax.div(request, each)
    distance = lax.shift_right_logical(device, 1) ^ chip
    return ((device & 1) ^ core) * kept + distance * each + lax.rem(request, each)


def parcel_kernel(
    mask_hbm, keys_hbm, values_hbm, query_hbm, blocks_ref, queries_ref, mask_ref, query, pad, sems
):
    held, rows = keys_hbm.shape[:2]
    pairs = [
        (mask_hbm, mask_ref),
        (query_hbm, query),
        (keys_hbm, blocks_ref.at[:, pl.ds(0, rows)]),
        (values_hbm, blocks_ref.at[:, pl.ds(rows, rows)]),
    ]
    copies = start_copies(pairs, sems)
    pad[...] = jnp.zeros_like(pad)
    for copy in copies:
        copy.wait()
    at = lax.broadcasted_iota(jnp.int32, (16, 128), 0) + lax.broadcasted_iota(
        jnp.int32, (16, 128), 1
    )
    for i in range(held):
        keys = blocks_ref[i, :16, :128].astype(F32)
        dead = mask_ref[0, i] != 1
        blocks_ref[i, :16, :128] = jnp.where((at == 0) & dead, DEAD_MARK, keys).astype(BF16)
    count, each = query.shape[1:3]
    for n in range(count):
        pair = query[0, n].astype(F32) * HEAD_SIZE**-0.5
        for k in range(each):
            pad[k, n : n + 1] = pair[k : k + 1]
    for k in range(each):
        queries_ref[k] = pack_rows(format_queries(pad[k])).astype(BF16)


def pair_kernel(own_ref, sibling_ref, out_ref):
    half = own_ref.shape[0]
    out_ref[:half] = own_ref[...]
    out_ref[half:] = sibling_ref[...]


def gather_kernel(*refs):
    for i, ref in enumerate(refs[:-1]):
        refs[-1][i] = ref[...]


def own_kernel(chips, each, shifts, held, *refs):
    owner_hbm, length_hbm, accepted_hbm, group_hbm = refs[:4]
    near_hbm, (keys_hbm, values_hbm) = refs[4:8], refs[8:10]
    query_ref, own_out, table_out, keys_out, values_out = refs[10:15]
    owner_ref, length_ref, accepted_ref, group_ref = refs[15:19]
    owner_row, near, rows_ref, small_sems, piece_sems = refs[19:]
    pieces, rows = keys_out.shape[:2]
    kept = chips * each
    small = start_copies(
        [
            (owner_hbm, owner_ref),
            (length_hbm, length_ref),
            (accepted_hbm, accepted_ref),
            (group_hbm, group_ref),
            (owner_hbm, owner_row),
        ]
        + [(x.at[0], near.at[j]) for j, x in enumerate(near_hbm)],
        small_sems,
    )
    large = start_copies(
        [(keys_hbm.at[0, i], keys_out.at[i]) for i in range(pieces)]
        + [(values_hbm.at[0, i], values_out.at[i]) for i in range(pieces)],
        piece_sems,
    )
    me = lax.axis_index("blk")
    z = lax.axis_index("req")
    chip, core = lax.shift_right_logical(me, 1), me & 1
    rows_ref[...] = jnp.zeros_like(rows_ref)
    for copy in small:
        copy.wait()
    count = near.shape[1]
    for n in range(count):
        for j in range(4):
            pair = near[j, n].astype(F32)
            for k in range(each):
                to = (j % 2) * POSITIONS + n
                rows_ref[j // 2, k, to : to + 1] = pair[k : k + 1]

    shape = (KEY_HEADS * ROWS, 2 * POSITIONS)
    column = lax.broadcasted_iota(jnp.int32, shape, 1)
    position = lax.broadcasted_iota(jnp.int32, shape, 0) % POSITIONS
    for k in range(each):
        live = ((column < POSITIONS) & (column < accepted_ref[0, k])) | (
            (column >= POSITIONS)
            & (column < POSITIONS + count)
            & (column - POSITIONS <= position)
        )
        query = unpack_rows(query_ref[k].astype(F32)).astype(BF16)
        got = attend(query, rows_ref[0, k].astype(BF16), rows_ref[1, k].astype(BF16), live, False)
        for j in range(3):
            own_out[j, k] = got[j]

    owners = owner_row[...]
    slot = lax.broadcasted_iota(jnp.int32, owners.shape, 1)
    for i in range(pieces):
        index = me * pieces + i
        owner = owner_ref[0, index]
        same = jnp.where((owners == owner) & (slot < index), 1.0, 0.0)
        rank = jnp.sum(same, axis=1, keepdims=True).astype(jnp.int32)
        place = place_of(owner, each, chip, core, kept)
        table_out[i : i + 1] = jnp.full((1, 128), place, jnp.int32)
        table_out[pieces + i : pieces + i + 1] = jnp.broadcast_to(
            length_ref[0, owner] - rank * rows, (1, 128)
        )
    for i in range(kept):
        request = ((chip ^ (i // each)) * 2 + core) * each + i % each
        group = group_ref[0, request]
        shift = z ^ lax.div(group, held)
        array = jnp.where(shift < 2, shift, (shift & ~1) + ((shift ^ core ^ 1) & 1))
        to = 2 * pieces + i
        table_out[to : to + 1] = jnp.full((1, 128), array * held + lax.rem(group, held), jnp.int32)
    for copy in large:
        copy.wait()


def pieces_kernel(chips, each, *refs):
    table_ref = refs[0]
    query_refs = refs[1 : 1 + chips]
    keys, values, mine_out = refs[1 + chips : 4 + chips]
    sibling_outs = refs[4 + chips : 6 + chips]
    queries_out, queries, acc = refs[6 + chips :]
    pieces, rows = keys.shape[0], keys.shape[1]
    kept = chips * each
    core = lax.axis_index("blk") & 1
    for j in range(chips):
        distance = jnp.where(core == 0, j, across_cores(j, chips))
        handed = j > 0 and j < chips - 1 and j % 2 == 0
        for side in range(2):
            start = (1 - side if handed else side) * each
            for k in range(each):
                query = unpack_rows(query_refs[j][start + k].astype(F32))
                queries[side * kept + distance * each + k] = query.astype(BF16)
    queries_out[...] = queries[:kept]
    lane = lax.broadcasted_iota(jnp.int32, (1, rows), 1)
    places = [jnp.max(table_ref[i : i + 1]) for i in range(pieces)]
    got = []
    for i in range(pieces):
        filled = table_ref[pieces + i : pieces + i + 1]
        live = lane < jnp.concatenate([filled] * (rows // 128), axis=1)
        got.append(attend(queries[places[i]], keys[i], values[i], live, True))
    acc[0] = jnp.full_like(acc[0], LOWEST)
    acc[1] = jnp.zeros_like(acc[1])
    acc[2] = jnp.zeros_like(acc[2])
    for i in range(pieces):
        acc[0, places[i]] = jnp.maximum(acc[0, places[i]], got[i][0])
    for i in range(pieces):
        lift = jnp.exp(got[i][0] - acc[0, places[i]])
        acc[1, places[i]] += lift * got[i][1]
        acc[2, places[i]] += lift * got[i][2]
    mine_out[...] = acc[:, :kept]
    for i in range(kept):
        half, at = divmod(i, kept // 2)
        sibling_outs[half][at] = pack_message(*[acc[j, kept + i] for j in range(3)])


def join_kernel(mine_ref, own_ref, first_ref, second_ref, out_ref):
    half, each = first_ref.shape[0], own_ref.shape[1]
    opened = open_messages([first_ref[i] for i in range(half)] + [second_ref[i] for i in range(half)])
    for i in range(2 * half):
        blocks = [[mine_ref[j, i] for j in range(3)], opened[i]]
        if i < each:
            blocks.append([own_ref[j, i] for j in range(3)])
        joined = merge(*blocks)
        for j in range(3):
            out_ref[j, i] = joined[j]


def prompts_kernel(chips, each, first_row, *refs):
    table_ref, query_ref, joined_ref = refs[:3]
    own_ref, sibling_ref, fetched_ref, swapped_ref = refs[3:7]
    out_refs = refs[7:]
    held, rows = own_ref.shape[0], own_ref.shape[1] // 2
    far = fetched_ref.shape[0] - 1
    pairs = [
        (lambda i: own_ref[i], lambda i: sibling_ref[i]),
        (lambda i: fetched_ref[far, i], lambda i: swapped_ref[far, i]),
    ]
    for p in range(0, far, 2):
        for ref in (fetched_ref, swapped_ref):
            pairs.append(tuple(lambda i, ref=ref, at=p + side: ref[at, i] for side in range(2)))
    lane = lax.broadcasted_iota(jnp.int32, (1, 2 * rows), 1)
    got = []
    for i in range(chips * each):
        at = jnp.max(table_ref[first_row + i : first_row + i + 1])
        array, slot = lax.div(at, held), lax.rem(at, held)

        def block(side):
            out = pairs[0][side](slot)
            for j in range(1, len(pairs)):
                out = jnp.where(array == j, pairs[j][side](slot), out)
            return out

        mine, other = block(0), block(1)
        marks = jnp.where(lane < rows, mine[:1, :1].astype(F32), other[:1, :1].astype(F32))
        got.append(
            attend(
                query_ref[i],
                jnp.concatenate([mine[:rows], other[:rows]], axis=0),
                jnp.concatenate([mine[rows:], other[rows:]], axis=0),
                marks < 0.5 * DEAD_MARK,
                False,
            )
        )
    for i in range(chips * each):
        merged = merge([joined_ref[j, i] for j in range(3)], got[i])
        out_refs[i // each][i % each] = pack_message(*merged)


def combine_kernel(chips, *refs):
    message_refs, out_ref = refs[:chips], refs[chips]
    count, each = out_ref.shape[1], out_ref.shape[2]
    low = lax.broadcasted_iota(jnp.int32, (POSITIONS, 128), 1) < HEAD_SIZE
    rows = []
    opened = open_messages([ref[k] for k in range(each) for ref in message_refs])
    for k in range(each):
        _, mass, part = merge(*opened[k * chips : (k + 1) * chips])
        out = part / mass
        swapped = swap_halves(out)
        columns = []
        for head in range(0, QUERY_HEADS, 2):
            c, g = head // GROUP, head % GROUP
            tile = slice((c // 2) * 128, (c // 2) * 128 + 128)
            first, second = (out, swapped) if c % 2 == 0 else (swapped, out)
            columns.append(
                jnp.where(
                    low,
                    first[g * POSITIONS : (g + 1) * POSITIONS, tile],
                    second[(g + 1) * POSITIONS : (g + 2) * POSITIONS, tile],
                )
            )
        rows.append(jnp.concatenate(columns, axis=1))
    for n in range(count):
        out_ref[0, n] = jnp.concatenate([row[n : n + 1] for row in rows], axis=0).astype(BF16)


HBM = pl.BlockSpec(memory_space=pltpu.HBM)
VMEM = pl.BlockSpec(memory_space=pltpu.VMEM)


def in_hbm(x):
    return pltpu.with_memory_space_constraint(x, pltpu.HBM)


def call(kernel, name, out_shape, in_specs, scratch=(), cost=0):
    many = isinstance(out_shape, (list, tuple))
    return pl.pallas_call(
        kernel,
        name=name,
        out_shape=out_shape,
        in_specs=in_specs,
        out_specs=[VMEM] * len(out_shape) if many else VMEM,
        scratch_shapes=list(scratch),
        cost_estimate=pl.CostEstimate(flops=0, bytes_accessed=cost, transcendentals=0),
        compiler_params=pltpu.CompilerParams(vmem_limit_bytes=VMEM_LIMIT),
    )


def per_device(
    devices,
    shifts,
    verified_queries,
    new_keys,
    verified_value_rows,
    prior_round_keys,
    prior_round_values,
    accepted,
    group_id,
    cache_len,
    slot_owner,
    piece_cache_keys,
    piece_cache_values,
    shared_prompt_keys,
    shared_prompt_values,
    prompt_mask,
):
    shape = jax.ShapeDtypeStruct
    each = verified_queries.shape[1]
    chips = devices // 2
    pieces, piece_rows = piece_cache_keys.shape[1:3]
    held, block_rows = shared_prompt_keys.shape[:2]
    kept = chips * each

    def other_core(x):
        return lax.ppermute(x, "blk", [(i, i ^ 1) for i in range(devices)])

    def other_chip(x, s):
        return lax.ppermute(x, "blk", [(i, i ^ (2 * s)) for i in range(devices)])

    def along_req(x, even, odd):
        pairs = []
        for i in range(devices * shifts):
            d, z = divmod(i, shifts)
            pairs.append((i, d * shifts + (z ^ (odd if d % 2 else even))))
        return lax.ppermute(x, ("blk", "req"), pairs)

    verified_queries, prior_round_keys, new_keys, prior_round_values, verified_value_rows = (
        jnp.transpose(x, (0, 2, 1, 3))
        for x in (
            verified_queries, prior_round_keys, new_keys, prior_round_values, verified_value_rows,
        )
    )
    near = (prior_round_keys, new_keys, prior_round_values, verified_value_rows)
    count = verified_queries.shape[1]
    block_size = 2 * block_rows
    piece_shape = (pieces, piece_rows, WIDTH)
    own_blocks, own_queries = call(
        parcel_kernel,
        "parcel",
        [
            shape((held, block_size, WIDTH), BF16),
            shape((each, MESSAGE, WIDTH), BF16),
        ],
        [HBM] * 4,
        [
            pltpu.SMEM((1, held), jnp.int32),
            pltpu.VMEM(verified_queries.shape, BF16),
            pltpu.VMEM((each, POSITIONS, QUERY_HEADS * HEAD_SIZE), F32),
            pltpu.SemaphoreType.DMA((4,)),
        ],
    )(
        *(
            in_hbm(x)
            for x in (prompt_mask.T, shared_prompt_keys, shared_prompt_values, verified_queries)
        )
    )
    sibling_blocks, sibling_queries, later_blocks = lax.optimization_barrier(
        (other_core(own_blocks), other_core(own_queries), own_blocks)
    )
    fetched = []
    for s in range(2, shifts, 2):
        fetched += [along_req(x, s + 1, s) for x in (own_blocks, sibling_blocks)]
    fetched.append(along_req(later_blocks, 1, 1))
    chip_queries = call(
        pair_kernel, "pair", shape((2 * each, MESSAGE, WIDTH), BF16), [VMEM] * 2
    )(own_queries, sibling_queries)

    own, table, keys, values = call(
        functools.partial(own_kernel, chips, each, shifts, held),
        "own",
        [
            shape((3, each, ROWS, WIDTH), F32),
            shape((2 * pieces + kept, 128), jnp.int32),
            shape(piece_shape, BF16),
            shape(piece_shape, BF16),
        ],
        [HBM] * 10 + [VMEM],
        [
            pltpu.SMEM(slot_owner.shape, jnp.int32),
            pltpu.SMEM(cache_len.shape, jnp.int32),
            pltpu.SMEM(accepted.shape, jnp.int32),
            pltpu.SMEM(group_id.shape, jnp.int32),
            pltpu.VMEM(slot_owner.shape, jnp.int32),
            pltpu.VMEM((4, count, each, WIDTH), BF16),
            pltpu.VMEM((2, each, 2 * POSITIONS, WIDTH), F32),
            pltpu.SemaphoreType.DMA((9,)),
            pltpu.SemaphoreType.DMA((2 * pieces,)),
        ],
        8 * 1024 * 1024,
    )(
        *(
            in_hbm(x)
            for x in (slot_owner, cache_len, accepted, group_id)
            + near
            + (piece_cache_keys, piece_cache_values)
        ),
        chip_queries,
    )

    queries = [chip_queries]
    for s in range(1, chips - 1, 2):
        taken = lax.ppermute(
            chip_queries,
            "blk",
            [(i, i ^ (2 * (across_cores(s, chips) if i % 2 else s))) for i in range(devices)],
        )
        taken = lax.optimization_barrier((taken, table))[0]
        queries += [taken, other_core(taken)]
    if chips > 1:
        queries.append(other_chip(chip_queries, chips - 1))

    wide = (kept, ROWS, WIDTH)
    mine, *to_sibling, kept_queries = call(
        functools.partial(pieces_kernel, chips, each),
        "pieces",
        [shape((3,) + wide, F32)]
        + [shape((kept // 2, MESSAGE, WIDTH), F32)] * 2
        + [shape(wide, BF16)],
        [VMEM] * (chips + 3),
        [
            pltpu.VMEM((2 * kept, ROWS, WIDTH), BF16),
            pltpu.VMEM((3, 2 * kept, ROWS, WIDTH), F32),
        ],
    )(table, *queries, keys, values)
    from_sibling = [other_core(x) for x in to_sibling]
    joined = call(join_kernel, "join", shape((3,) + wide, F32), [VMEM] * 4)(
        mine, own, *from_sibling
    )
    fetched = lax.optimization_barrier((kept_queries, *fetched))[1:]
    gathered = call(
        gather_kernel,
        "gather",
        shape((len(fetched), held, block_size, WIDTH), BF16),
        [VMEM] * len(fetched),
    )(*fetched)

    messages = call(
        functools.partial(prompts_kernel, chips, each, 2 * pieces),
        "prompts",
        [shape((each, MESSAGE, WIDTH), F32)] * chips,
        [VMEM] * 7,
    )(table, kept_queries, joined, own_blocks, sibling_blocks, gathered, other_core(gathered))
    arrived = [messages[0]] + [other_chip(messages[s], s) for s in range(chips - 1, 0, -1)]

    out = call(
        functools.partial(combine_kernel, chips),
        "combine",
        shape(verified_queries.shape, BF16),
        [VMEM] * chips,
    )(*arrived)
    return jnp.transpose(out, (0, 2, 1, 3))


def solution(mesh):
    placed = (
        P("req", "blk", None, None),
        P("req", "blk", None, None),
        P("req", "blk", None, None),
        P("req", "blk", None, None),
        P("req", "blk", None, None),
        P("req", "blk"),
        P("req", None),
        P("req", None),
        P("req", None),
        P("req", "blk", None, None),
        P("req", "blk", None, None),
        P("req", "blk", None),
        P("req", "blk", None),
        P("req", "blk"),
    )
    return jax.shard_map(
        functools.partial(per_device, mesh.shape["blk"], mesh.shape["req"]),
        mesh=mesh,
        in_specs=placed,
        out_specs=P("req", "blk", None, None),
        check_vma=False,
    )
```

```python
import functools

import jax
import jax.numpy as jnp
from jax import lax
from jax.experimental import pallas as pl
from jax.experimental.pallas import tpu as pltpu
from jax.sharding import PartitionSpec as P

QUERY_HEADS = 16
KEY_HEADS = 4
HEAD_SIZE = 64
GROUP = QUERY_HEADS // KEY_HEADS
POSITIONS = 8
ROWS = GROUP * POSITIONS
WIDTH = KEY_HEADS * HEAD_SIZE
MESSAGE = 3 * POSITIONS

LOWEST = float(jnp.bfloat16(-1e30))
DEAD_MARK = 64.0

F32 = jnp.float32
BF16 = jnp.bfloat16
VMEM_LIMIT = 48 * 1024 * 1024


def head_of_lane(shape):
    return lax.broadcasted_iota(jnp.int32, shape, len(shape) - 1) // HEAD_SIZE


def swap_halves(x):
    pieces = [pltpu.roll(x[:, i : i + 128], HEAD_SIZE, 1) for i in range(0, x.shape[1], 128)]
    return jnp.concatenate(pieces, axis=1)


def spread_queries(q):
    lanes = head_of_lane(q.shape)
    zero = jnp.zeros_like(q)
    return jnp.concatenate([jnp.where(lanes == c, q, zero) for c in range(KEY_HEADS)], axis=0)


def fold_heads(x):
    lanes = head_of_lane((ROWS, WIDTH))
    out = jnp.broadcast_to(x[:ROWS], (ROWS, WIDTH))
    for c in range(1, KEY_HEADS):
        out = jnp.where(lanes == c, x[c * ROWS : (c + 1) * ROWS], out)
    return out


def score(q, keys):
    return lax.dot_general(
        spread_queries(q), keys, (((1,), (1,)), ((), ())), preferred_element_type=F32
    )


def attend(q, keys, values, live, wide):
    masked = jnp.where(live, score(q, keys), LOWEST)
    top = jnp.max(masked, axis=1, keepdims=True)
    weights = jnp.exp(masked - top).astype(BF16)
    if wide:
        values = jnp.concatenate([values, jnp.ones((values.shape[0], 128), BF16)], axis=1)
    part = jnp.dot(weights, values, preferred_element_type=F32)
    if wide:
        mass = jnp.concatenate([part[:, WIDTH:]] * 2, axis=1)
    else:
        mass = jnp.sum(weights.astype(F32), axis=1, keepdims=True)
    return fold_heads(top), fold_heads(mass), fold_heads(part[:, :WIDTH])


def merge(*blocks):
    top = functools.reduce(jnp.maximum, [b[0] for b in blocks])
    lifts = [jnp.exp(b[0] - top) for b in blocks]
    mass = functools.reduce(jnp.add, [a * b[1] for a, b in zip(lifts, blocks)])
    part = functools.reduce(jnp.add, [a * b[2] for a, b in zip(lifts, blocks)])
    return top, mass, part


def spot(shape):
    lane = lax.broadcasted_iota(jnp.int32, shape, 1) % HEAD_SIZE
    return lane == lax.broadcasted_iota(jnp.int32, shape, 0) % ROWS


def pack_rows(x, spare=(None, None, None)):
    sub = lax.broadcasted_iota(jnp.int32, (POSITIONS, WIDTH), 0)
    tile = lambda i: x[i * POSITIONS : (i + 1) * POSITIONS]
    a, b, c = (jnp.zeros((1, WIDTH), x.dtype) if row is None else row for row in spare)
    return jnp.concatenate(
        [
            jnp.where(sub < 5, tile(0), pltpu.roll(tile(3), 5, 0)),
            jnp.where(sub < 5, tile(1), jnp.where(sub < 7, pltpu.roll(tile(3), 2, 0), a)),
            jnp.where(sub < 5, tile(2), jnp.where(sub < 6, b, c)),
        ],
        axis=0,
    )


def unpack_rows(x):
    sub = lax.broadcasted_iota(jnp.int32, (POSITIONS, WIDTH), 0)
    last = jnp.where(sub < 3, pltpu.roll(x[0:8], 3, 0), pltpu.roll(x[8:16], 6, 0))
    return jnp.concatenate([x, last], axis=0)


def pack_message(top, mass, part):
    rounded = top.astype(BF16).astype(F32)
    lift = jnp.exp(top - rounded)
    mass, part = mass * lift, part * lift
    high = mass.astype(BF16).astype(F32)
    at = spot((ROWS, WIDTH))
    row_of = lambda x: jnp.sum(jnp.where(at, x, 0.0), axis=0, keepdims=True)
    return pack_rows(part, (row_of(rounded), row_of(high), row_of(mass - high)))


def open_messages(messages):
    at = spot((ROWS, WIDTH))
    rows = []
    for x in messages:
        for r in (15, 21, 22):
            rows.append(jnp.where(at, x[r : r + 1], 0.0).astype(BF16))
    same_head = lax.broadcasted_iota(jnp.int32, (WIDTH, WIDTH), 0) // HEAD_SIZE == (
        lax.broadcasted_iota(jnp.int32, (WIDTH, WIDTH), 1) // HEAD_SIZE
    )
    ones = jnp.where(same_head, 1.0, 0.0).astype(BF16)
    spread = jnp.dot(jnp.concatenate(rows, axis=0), ones, preferred_element_type=F32)
    out = []
    for i, x in enumerate(messages):
        get = lambda j: spread[(3 * i + j) * ROWS : (3 * i + j + 1) * ROWS]
        out.append((get(0), get(1) + get(2), unpack_rows(x)))
    return out


def start_copies(pairs, sems):
    copies = [
        pltpu.make_async_copy(source, target, sems.at[i]) for i, (source, target) in enumerate(pairs)
    ]
    for copy in copies:
        copy.start()
    return copies


def format_queries(q):
    low = lax.broadcasted_iota(jnp.int32, (POSITIONS, 128), 1) < HEAD_SIZE
    swapped = swap_halves(q)
    rows = []
    for g in range(GROUP):
        columns = []
        for c in range(0, KEY_HEADS, 2):
            halves = []
            for half in range(2):
                tile = (GROUP * (c + half) + g) // 2
                array = q if g % 2 == half else swapped
                halves.append(array[:, tile * 128 : tile * 128 + 128])
            columns.append(jnp.where(low, halves[0], halves[1]))
        rows.append(jnp.concatenate(columns, axis=1))
    return jnp.concatenate(rows, axis=0)


def across_cores(j, chips):
    if j == 0 or j == chips - 1:
        return j
    return j + 1 if j % 2 else j - 1


def place_of(request, each, chip, core, kept):
    device = lax.div(request, each)
    distance = lax.shift_right_logical(device, 1) ^ chip
    return ((device & 1) ^ core) * kept + distance * each + lax.rem(request, each)


def parcel_kernel(
    mask_hbm, keys_hbm, values_hbm, query_hbm, blocks_ref, queries_ref, mask_ref, query, pad, sems
):
    held, rows = keys_hbm.shape[:2]
    pairs = [
        (mask_hbm, mask_ref),
        (query_hbm, query),
        (keys_hbm, blocks_ref.at[:, pl.ds(0, rows)]),
        (values_hbm, blocks_ref.at[:, pl.ds(rows, rows)]),
    ]
    copies = start_copies(pairs, sems)
    pad[...] = jnp.zeros_like(pad)
    for copy in copies:
        copy.wait()
    at = lax.broadcasted_iota(jnp.int32, (16, 128), 0) + lax.broadcasted_iota(
        jnp.int32, (16, 128), 1
    )
    for i in range(held):
        keys = blocks_ref[i, :16, :128].astype(F32)
        dead = mask_ref[0, i] != 1
        blocks_ref[i, :16, :128] = jnp.where((at == 0) & dead, DEAD_MARK, keys).astype(BF16)
    count, each = query.shape[1:3]
    for n in range(count):
        pair = query[0, n].astype(F32) * HEAD_SIZE**-0.5
        for k in range(each):
            pad[k, n : n + 1] = pair[k : k + 1]
    for k in range(each):
        queries_ref[k] = pack_rows(format_queries(pad[k])).astype(BF16)


def pair_kernel(own_ref, sibling_ref, out_ref):
    half = own_ref.shape[0]
    out_ref[:half] = own_ref[...]
    out_ref[half:] = sibling_ref[...]


def gather_kernel(*refs):
    for i, ref in enumerate(refs[:-1]):
        refs[-1][i] = ref[...]


def own_kernel(chips, each, shifts, held, *refs):
    owner_hbm, length_hbm, accepted_hbm, group_hbm = refs[:4]
    near_hbm, (keys_hbm, values_hbm) = refs[4:8], refs[8:10]
    query_ref, own_out, table_out, keys_out, values_out = refs[10:15]
    owner_ref, length_ref, accepted_ref, group_ref = refs[15:19]
    owner_row, near, rows_ref, small_sems, piece_sems = refs[19:]
    pieces, rows = keys_out.shape[:2]
    kept = chips * each
    small = start_copies(
        [
            (owner_hbm, owner_ref),
            (length_hbm, length_ref),
            (accepted_hbm, accepted_ref),
            (group_hbm, group_ref),
            (owner_hbm, owner_row),
        ]
        + [(x.at[0], near.at[j]) for j, x in enumerate(near_hbm)],
        small_sems,
    )
    large = start_copies(
        [(keys_hbm.at[0, i], keys_out.at[i]) for i in range(pieces)]
        + [(values_hbm.at[0, i], values_out.at[i]) for i in range(pieces)],
        piece_sems,
    )
    me = lax.axis_index("blk")
    z = lax.axis_index("req")
    chip, core = lax.shift_right_logical(me, 1), me & 1
    rows_ref[...] = jnp.zeros_like(rows_ref)
    for copy in small:
        copy.wait()
    count = near.shape[1]
    for n in range(count):
        for j in range(4):
            pair = near[j, n].astype(F32)
            for k in range(each):
                to = (j % 2) * POSITIONS + n
                rows_ref[j // 2, k, to : to + 1] = pair[k : k + 1]

    shape = (KEY_HEADS * ROWS, 2 * POSITIONS)
    column = lax.broadcasted_iota(jnp.int32, shape, 1)
    position = lax.broadcasted_iota(jnp.int32, shape, 0) % POSITIONS
    for k in range(each):
        live = ((column < POSITIONS) & (column < accepted_ref[0, k])) | (
            (column >= POSITIONS)
            & (column < POSITIONS + count)
            & (column - POSITIONS <= position)
        )
        query = unpack_rows(query_ref[k].astype(F32)).astype(BF16)
        got = attend(query, rows_ref[0, k].astype(BF16), rows_ref[1, k].astype(BF16), live, True)
        for j in range(3):
            own_out[j, k] = got[j]

    owners = owner_row[...]
    slot = lax.broadcasted_iota(jnp.int32, owners.shape, 1)
    for i in range(pieces):
        index = me * pieces + i
        owner = owner_ref[0, index]
        same = jnp.where((owners == owner) & (slot < index), 1.0, 0.0)
        rank = jnp.sum(same, axis=1, keepdims=True).astype(jnp.int32)
        place = place_of(owner, each, chip, core, kept)
        table_out[i : i + 1] = jnp.full((1, 128), place, jnp.int32)
        table_out[pieces + i : pieces + i + 1] = jnp.broadcast_to(
            length_ref[0, owner] - rank * rows, (1, 128)
        )
    for i in range(kept):
        request = ((chip ^ (i // each)) * 2 + core) * each + i % each
        group = group_ref[0, request]
        shift = z ^ lax.div(group, held)
        array = jnp.where(shift < 2, shift, (shift & ~1) + ((shift ^ core ^ 1) & 1))
        to = 2 * pieces + i
        table_out[to : to + 1] = jnp.full((1, 128), array * held + lax.rem(group, held), jnp.int32)
    for copy in large:
        copy.wait()


def pieces_kernel(chips, each, *refs):
    table_ref = refs[0]
    query_refs = refs[1 : 1 + chips]
    keys, values, mine_out = refs[1 + chips : 4 + chips]
    sibling_outs = refs[4 + chips : 6 + chips]
    queries_out, queries, acc = refs[6 + chips :]
    pieces, rows = keys.shape[0], keys.shape[1]
    kept = chips * each
    core = lax.axis_index("blk") & 1
    for j in range(chips):
        distance = jnp.where(core == 0, j, across_cores(j, chips))
        handed = j > 0 and j < chips - 1 and j % 2 == 0
        for side in range(2):
            start = (1 - side if handed else side) * each
            for k in range(each):
                query = unpack_rows(query_refs[j][start + k].astype(F32))
                queries[side * kept + distance * each + k] = query.astype(BF16)
    queries_out[...] = queries[:kept]
    lane = lax.broadcasted_iota(jnp.int32, (1, rows), 1)
    places = [jnp.max(table_ref[i : i + 1]) for i in range(pieces)]
    got = []
    for i in range(pieces):
        filled = table_ref[pieces + i : pieces + i + 1]
        live = lane < jnp.concatenate([filled] * (rows // 128), axis=1)
        got.append(attend(queries[places[i]], keys[i], values[i], live, True))
    acc[0] = jnp.full_like(acc[0], LOWEST)
    acc[1] = jnp.zeros_like(acc[1])
    acc[2] = jnp.zeros_like(acc[2])
    for i in range(pieces):
        acc[0, places[i]] = jnp.maximum(acc[0, places[i]], got[i][0])
    for i in range(pieces):
        lift = jnp.exp(got[i][0] - acc[0, places[i]])
        acc[1, places[i]] += lift * got[i][1]
        acc[2, places[i]] += lift * got[i][2]
    mine_out[...] = acc[:, :kept]
    for i in range(kept):
        half, at = divmod(i, kept // 2)
        sibling_outs[half][at] = pack_message(*[acc[j, kept + i] for j in range(3)])


def join_kernel(mine_ref, own_ref, first_ref, second_ref, out_ref):
    half, each = first_ref.shape[0], own_ref.shape[1]
    opened = open_messages([first_ref[i] for i in range(half)] + [second_ref[i] for i in range(half)])
    for i in range(2 * half):
        blocks = [[mine_ref[j, i] for j in range(3)], opened[i]]
        if i < each:
            blocks.append([own_ref[j, i] for j in range(3)])
        joined = merge(*blocks)
        for j in range(3):
            out_ref[j, i] = joined[j]


def prompts_kernel(chips, each, first_row, *refs):
    table_ref, query_ref, joined_ref = refs[:3]
    own_ref, sibling_ref, fetched_ref, swapped_ref = refs[3:7]
    out_refs = refs[7:]
    held, rows = own_ref.shape[0], own_ref.shape[1] // 2
    far = fetched_ref.shape[0] - 1
    pairs = [
        (lambda i: own_ref[i], lambda i: sibling_ref[i]),
        (lambda i: fetched_ref[far, i], lambda i: swapped_ref[far, i]),
    ]
    for p in range(0, far, 2):
        for ref in (fetched_ref, swapped_ref):
            pairs.append(tuple(lambda i, ref=ref, at=p + side: ref[at, i] for side in range(2)))
    lane = lax.broadcasted_iota(jnp.int32, (1, 2 * rows), 1)
    got = []
    for i in range(chips * each):
        at = jnp.max(table_ref[first_row + i : first_row + i + 1])
        array, slot = lax.div(at, held), lax.rem(at, held)

        def block(side):
            out = pairs[0][side](slot)
            for j in range(1, len(pairs)):
                out = jnp.where(array == j, pairs[j][side](slot), out)
            return out

        mine, other = block(0), block(1)
        marks = jnp.where(lane < rows, mine[:1, :1].astype(F32), other[:1, :1].astype(F32))
        got.append(
            attend(
                query_ref[i],
                jnp.concatenate([mine[:rows], other[:rows]], axis=0),
                jnp.concatenate([mine[rows:], other[rows:]], axis=0),
                marks < 0.5 * DEAD_MARK,
                False,
            )
        )
    for i in range(chips * each):
        merged = merge([joined_ref[j, i] for j in range(3)], got[i])
        out_refs[i // each][i % each] = pack_message(*merged)


def combine_kernel(chips, *refs):
    message_refs, out_ref = refs[:chips], refs[chips]
    count, each = out_ref.shape[1], out_ref.shape[2]
    low = lax.broadcasted_iota(jnp.int32, (POSITIONS, 128), 1) < HEAD_SIZE
    rows = []
    opened = open_messages([ref[k] for k in range(each) for ref in message_refs])
    for k in range(each):
        _, mass, part = merge(*opened[k * chips : (k + 1) * chips])
        out = part / mass
        swapped = swap_halves(out)
        columns = []
        for head in range(0, QUERY_HEADS, 2):
            c, g = head // GROUP, head % GROUP
            tile = slice((c // 2) * 128, (c // 2) * 128 + 128)
            first, second = (out, swapped) if c % 2 == 0 else (swapped, out)
            columns.append(
                jnp.where(
                    low,
                    first[g * POSITIONS : (g + 1) * POSITIONS, tile],
                    second[(g + 1) * POSITIONS : (g + 2) * POSITIONS, tile],
                )
            )
        rows.append(jnp.concatenate(columns, axis=1))
    for n in range(count):
        out_ref[0, n] = jnp.concatenate([row[n : n + 1] for row in rows], axis=0).astype(BF16)


HBM = pl.BlockSpec(memory_space=pltpu.HBM)
VMEM = pl.BlockSpec(memory_space=pltpu.VMEM)


def in_hbm(x):
    return pltpu.with_memory_space_constraint(x, pltpu.HBM)


def call(kernel, name, out_shape, in_specs, scratch=(), cost=0):
    many = isinstance(out_shape, (list, tuple))
    return pl.pallas_call(
        kernel,
        name=name,
        out_shape=out_shape,
        in_specs=in_specs,
        out_specs=[VMEM] * len(out_shape) if many else VMEM,
        scratch_shapes=list(scratch),
        cost_estimate=pl.CostEstimate(flops=0, bytes_accessed=cost, transcendentals=0),
        compiler_params=pltpu.CompilerParams(vmem_limit_bytes=VMEM_LIMIT),
    )


def per_device(
    devices,
    shifts,
    verified_queries,
    new_keys,
    verified_value_rows,
    prior_round_keys,
    prior_round_values,
    accepted,
    group_id,
    cache_len,
    slot_owner,
    piece_cache_keys,
    piece_cache_values,
    shared_prompt_keys,
    shared_prompt_values,
    prompt_mask,
):
    shape = jax.ShapeDtypeStruct
    each = verified_queries.shape[1]
    chips = devices // 2
    pieces, piece_rows = piece_cache_keys.shape[1:3]
    held, block_rows = shared_prompt_keys.shape[:2]
    kept = chips * each

    def other_core(x):
        return lax.ppermute(x, "blk", [(i, i ^ 1) for i in range(devices)])

    def other_chip(x, s):
        return lax.ppermute(x, "blk", [(i, i ^ (2 * s)) for i in range(devices)])

    def along_req(x, even, odd):
        pairs = []
        for i in range(devices * shifts):
            d, z = divmod(i, shifts)
            pairs.append((i, d * shifts + (z ^ (odd if d % 2 else even))))
        return lax.ppermute(x, ("blk", "req"), pairs)

    verified_queries, prior_round_keys, new_keys, prior_round_values, verified_value_rows = (
        jnp.transpose(x, (0, 2, 1, 3))
        for x in (
            verified_queries, prior_round_keys, new_keys, prior_round_values, verified_value_rows,
        )
    )
    near = (prior_round_keys, new_keys, prior_round_values, verified_value_rows)
    count = verified_queries.shape[1]
    block_size = 2 * block_rows
    piece_shape = (pieces, piece_rows, WIDTH)
    own_blocks, own_queries = call(
        parcel_kernel,
        "parcel",
        [
            shape((held, block_size, WIDTH), BF16),
            shape((each, MESSAGE, WIDTH), BF16),
        ],
        [HBM] * 4,
        [
            pltpu.SMEM((1, held), jnp.int32),
            pltpu.VMEM(verified_queries.shape, BF16),
            pltpu.VMEM((each, POSITIONS, QUERY_HEADS * HEAD_SIZE), F32),
            pltpu.SemaphoreType.DMA((4,)),
        ],
    )(
        *(
            in_hbm(x)
            for x in (prompt_mask.T, shared_prompt_keys, shared_prompt_values, verified_queries)
        )
    )
    sibling_blocks, sibling_queries, later_blocks = lax.optimization_barrier(
        (other_core(own_blocks), other_core(own_queries), own_blocks)
    )
    fetched = []
    for s in range(2, shifts, 2):
        fetched += [along_req(x, s + 1, s) for x in (own_blocks, sibling_blocks)]
    fetched.append(along_req(later_blocks, 1, 1))
    chip_queries = call(
        pair_kernel, "pair", shape((2 * each, MESSAGE, WIDTH), BF16), [VMEM] * 2
    )(own_queries, sibling_queries)

    own, table, keys, values = call(
        functools.partial(own_kernel, chips, each, shifts, held),
        "own",
        [
            shape((3, each, ROWS, WIDTH), F32),
            shape((2 * pieces + kept, 128), jnp.int32),
            shape(piece_shape, BF16),
            shape(piece_shape, BF16),
        ],
        [HBM] * 10 + [VMEM],
        [
            pltpu.SMEM(slot_owner.shape, jnp.int32),
            pltpu.SMEM(cache_len.shape, jnp.int32),
            pltpu.SMEM(accepted.shape, jnp.int32),
            pltpu.SMEM(group_id.shape, jnp.int32),
            pltpu.VMEM(slot_owner.shape, jnp.int32),
            pltpu.VMEM((4, count, each, WIDTH), BF16),
            pltpu.VMEM((2, each, 2 * POSITIONS, WIDTH), F32),
            pltpu.SemaphoreType.DMA((9,)),
            pltpu.SemaphoreType.DMA((2 * pieces,)),
        ],
        8 * 1024 * 1024,
    )(
        *(
            in_hbm(x)
            for x in (slot_owner, cache_len, accepted, group_id)
            + near
            + (piece_cache_keys, piece_cache_values)
        ),
        chip_queries,
    )

    queries = [chip_queries]
    for s in range(1, chips - 1, 2):
        taken = lax.ppermute(
            chip_queries,
            "blk",
            [(i, i ^ (2 * (across_cores(s, chips) if i % 2 else s))) for i in range(devices)],
        )
        taken = lax.optimization_barrier((taken, table))[0]
        queries += [taken, other_core(taken)]
    if chips > 1:
        queries.append(other_chip(chip_queries, chips - 1))

    wide = (kept, ROWS, WIDTH)
    mine, *to_sibling, kept_queries = call(
        functools.partial(pieces_kernel, chips, each),
        "pieces",
        [shape((3,) + wide, F32)]
        + [shape((kept // 2, MESSAGE, WIDTH), F32)] * 2
        + [shape(wide, BF16)],
        [VMEM] * (chips + 3),
        [
            pltpu.VMEM((2 * kept, ROWS, WIDTH), BF16),
            pltpu.VMEM((3, 2 * kept, ROWS, WIDTH), F32),
        ],
    )(table, *queries, keys, values)
    from_sibling = [other_core(x) for x in to_sibling]
    joined = call(join_kernel, "join", shape((3,) + wide, F32), [VMEM] * 4)(
        mine, own, *from_sibling
    )
    fetched = lax.optimization_barrier((kept_queries, *fetched))[1:]
    gathered = call(
        gather_kernel,
        "gather",
        shape((len(fetched), held, block_size, WIDTH), BF16),
        [VMEM] * len(fetched),
    )(*fetched)

    messages = call(
        functools.partial(prompts_kernel, chips, each, 2 * pieces),
        "prompts",
        [shape((each, MESSAGE, WIDTH), F32)] * chips,
        [VMEM] * 7,
    )(table, kept_queries, joined, own_blocks, sibling_blocks, gathered, other_core(gathered))
    arrived = [messages[0]] + [other_chip(messages[s], s) for s in range(chips - 1, 0, -1)]

    out = call(
        functools.partial(combine_kernel, chips),
        "combine",
        shape(verified_queries.shape, BF16),
        [VMEM] * chips,
    )(*arrived)
    return jnp.transpose(out, (0, 2, 1, 3))


def solution(mesh):
    placed = (
        P("req", "blk", None, None),
        P("req", "blk", None, None),
        P("req", "blk", None, None),
        P("req", "blk", None, None),
        P("req", "blk", None, None),
        P("req", "blk"),
        P("req", None),
        P("req", None),
        P("req", None),
        P("req", "blk", None, None),
        P("req", "blk", None, None),
        P("req", "blk", None),
        P("req", "blk", None),
        P("req", "blk"),
    )
    return jax.shard_map(
        functools.partial(per_device, mesh.shape["blk"], mesh.shape["req"]),
        mesh=mesh,
        in_specs=placed,
        out_specs=P("req", "blk", None, None),
        check_vma=False,
    )
```

```python
import functools

import jax
import jax.numpy as jnp
from jax import lax
from jax.experimental import pallas as pl
from jax.experimental.pallas import tpu as pltpu
from jax.sharding import PartitionSpec as P

QUERY_HEADS = 16
KEY_HEADS = 4
HEAD_SIZE = 64
GROUP = QUERY_HEADS // KEY_HEADS
POSITIONS = 8
ROWS = GROUP * POSITIONS
WIDTH = KEY_HEADS * HEAD_SIZE
MESSAGE = 3 * POSITIONS

LOWEST = float(jnp.bfloat16(-1e30))
DEAD_MARK = 64.0

F32 = jnp.float32
BF16 = jnp.bfloat16
VMEM_LIMIT = 48 * 1024 * 1024


def head_of_lane(shape):
    return lax.broadcasted_iota(jnp.int32, shape, len(shape) - 1) // HEAD_SIZE


def swap_halves(x):
    pieces = [pltpu.roll(x[:, i : i + 128], HEAD_SIZE, 1) for i in range(0, x.shape[1], 128)]
    return jnp.concatenate(pieces, axis=1)


def spread_queries(q):
    lanes = head_of_lane(q.shape)
    zero = jnp.zeros_like(q)
    return jnp.concatenate([jnp.where(lanes == c, q, zero) for c in range(KEY_HEADS)], axis=0)


def fold_heads(x):
    lanes = head_of_lane((ROWS, WIDTH))
    out = jnp.broadcast_to(x[:ROWS], (ROWS, WIDTH))
    for c in range(1, KEY_HEADS):
        out = jnp.where(lanes == c, x[c * ROWS : (c + 1) * ROWS], out)
    return out


def score(q, keys):
    return lax.dot_general(
        spread_queries(q), keys, (((1,), (1,)), ((), ())), preferred_element_type=F32
    )


def attend(q, keys, values, live, wide):
    masked = jnp.where(live, score(q, keys), LOWEST)
    top = jnp.max(masked, axis=1, keepdims=True)
    weights = jnp.exp(masked - top).astype(BF16)
    if wide:
        values = jnp.concatenate([values, jnp.ones((values.shape[0], 128), BF16)], axis=1)
    part = jnp.dot(weights, values, preferred_element_type=F32)
    if wide:
        mass = jnp.concatenate([part[:, WIDTH:]] * 2, axis=1)
    else:
        mass = jnp.sum(weights.astype(F32), axis=1, keepdims=True)
    return fold_heads(top), fold_heads(mass), fold_heads(part[:, :WIDTH])


def merge(*blocks):
    top = functools.reduce(jnp.maximum, [b[0] for b in blocks])
    lifts = [jnp.exp(b[0] - top) for b in blocks]
    mass = functools.reduce(jnp.add, [a * b[1] for a, b in zip(lifts, blocks)])
    part = functools.reduce(jnp.add, [a * b[2] for a, b in zip(lifts, blocks)])
    return top, mass, part


def spot(shape):
    lane = lax.broadcasted_iota(jnp.int32, shape, 1) % HEAD_SIZE
    return lane == lax.broadcasted_iota(jnp.int32, shape, 0) % ROWS


def pack_rows(x, spare=(None, None, None)):
    sub = lax.broadcasted_iota(jnp.int32, (POSITIONS, WIDTH), 0)
    tile = lambda i: x[i * POSITIONS : (i + 1) * POSITIONS]
    a, b, c = (jnp.zeros((1, WIDTH), x.dtype) if row is None else row for row in spare)
    return jnp.concatenate(
        [
            jnp.where(sub < 5, tile(0), pltpu.roll(tile(3), 5, 0)),
            jnp.where(sub < 5, tile(1), jnp.where(sub < 7, pltpu.roll(tile(3), 2, 0), a)),
            jnp.where(sub < 5, tile(2), jnp.where(sub < 6, b, c)),
        ],
        axis=0,
    )


def unpack_rows(x):
    sub = lax.broadcasted_iota(jnp.int32, (POSITIONS, WIDTH), 0)
    last = jnp.where(sub < 3, pltpu.roll(x[0:8], 3, 0), pltpu.roll(x[8:16], 6, 0))
    return jnp.concatenate([x, last], axis=0)


def pack_message(top, mass, part):
    rounded = top.astype(BF16).astype(F32)
    lift = jnp.exp(top - rounded)
    mass, part = mass * lift, part * lift
    high = mass.astype(BF16).astype(F32)
    at = spot((ROWS, WIDTH))
    row_of = lambda x: jnp.sum(jnp.where(at, x, 0.0), axis=0, keepdims=True)
    return pack_rows(part, (row_of(rounded), row_of(high), row_of(mass - high)))


def open_messages(messages):
    at = spot((ROWS, WIDTH))
    rows = []
    for x in messages:
        for r in (15, 21, 22):
            rows.append(jnp.where(at, x[r : r + 1], 0.0).astype(BF16))
    same_head = lax.broadcasted_iota(jnp.int32, (WIDTH, WIDTH), 0) // HEAD_SIZE == (
        lax.broadcasted_iota(jnp.int32, (WIDTH, WIDTH), 1) // HEAD_SIZE
    )
    ones = jnp.where(same_head, 1.0, 0.0).astype(BF16)
    spread = jnp.dot(jnp.concatenate(rows, axis=0), ones, preferred_element_type=F32)
    out = []
    for i, x in enumerate(messages):
        get = lambda j: spread[(3 * i + j) * ROWS : (3 * i + j + 1) * ROWS]
        out.append((get(0), get(1) + get(2), unpack_rows(x)))
    return out


def start_copies(pairs, sems):
    copies = [
        pltpu.make_async_copy(source, target, sems.at[i]) for i, (source, target) in enumerate(pairs)
    ]
    for copy in copies:
        copy.start()
    return copies


def format_queries(q):
    low = lax.broadcasted_iota(jnp.int32, (POSITIONS, 128), 1) < HEAD_SIZE
    swapped = swap_halves(q)
    rows = []
    for g in range(GROUP):
        columns = []
        for c in range(0, KEY_HEADS, 2):
            halves = []
            for half in range(2):
                tile = (GROUP * (c + half) + g) // 2
                array = q if g % 2 == half else swapped
                halves.append(array[:, tile * 128 : tile * 128 + 128])
            columns.append(jnp.where(low, halves[0], halves[1]))
        rows.append(jnp.concatenate(columns, axis=1))
    return jnp.concatenate(rows, axis=0)


def across_cores(j, chips):
    if j == 0 or j == chips - 1:
        return j
    return j + 1 if j % 2 else j - 1


def place_of(request, each, chip, core, kept):
    device = lax.div(request, each)
    distance = lax.shift_right_logical(device, 1) ^ chip
    return ((device & 1) ^ core) * kept + distance * each + lax.rem(request, each)


def parcel_kernel(
    mask_hbm, keys_hbm, values_hbm, query_hbm, blocks_ref, queries_ref, mask_ref, query, pad, sems
):
    held, rows = keys_hbm.shape[:2]
    pairs = [
        (mask_hbm, mask_ref),
        (query_hbm, query),
        (keys_hbm, blocks_ref.at[:, pl.ds(0, rows)]),
        (values_hbm, blocks_ref.at[:, pl.ds(rows, rows)]),
    ]
    copies = start_copies(pairs, sems)
    pad[...] = jnp.zeros_like(pad)
    for copy in copies:
        copy.wait()
    at = lax.broadcasted_iota(jnp.int32, (16, 128), 0) + lax.broadcasted_iota(
        jnp.int32, (16, 128), 1
    )
    for i in range(held):
        keys = blocks_ref[i, :16, :128].astype(F32)
        dead = mask_ref[0, i] != 1
        blocks_ref[i, :16, :128] = jnp.where((at == 0) & dead, DEAD_MARK, keys).astype(BF16)
    count, each = query.shape[1:3]
    for n in range(count):
        pair = query[0, n].astype(F32) * HEAD_SIZE**-0.5
        for k in range(each):
            pad[k, n : n + 1] = pair[k : k + 1]
    for k in range(each):
        queries_ref[k] = pack_rows(format_queries(pad[k])).astype(BF16)


def pair_kernel(own_ref, sibling_ref, out_ref):
    half = own_ref.shape[0]
    out_ref[:half] = own_ref[...]
    out_ref[half:] = sibling_ref[...]


def gather_kernel(*refs):
    for i, ref in enumerate(refs[:-1]):
        refs[-1][i] = ref[...]


def own_kernel(chips, each, shifts, held, *refs):
    owner_hbm, length_hbm, accepted_hbm, group_hbm = refs[:4]
    near_hbm, (keys_hbm, values_hbm) = refs[4:8], refs[8:10]
    query_ref, own_out, table_out, keys_out, values_out = refs[10:15]
    owner_ref, length_ref, accepted_ref, group_ref = refs[15:19]
    owner_row, near, rows_ref, small_sems, piece_sems = refs[19:]
    pieces, rows = keys_out.shape[:2]
    kept = chips * each
    small = start_copies(
        [
            (owner_hbm, owner_ref),
            (length_hbm, length_ref),
            (accepted_hbm, accepted_ref),
            (group_hbm, group_ref),
            (owner_hbm, owner_row),
        ]
        + [(x.at[0], near.at[j]) for j, x in enumerate(near_hbm)],
        small_sems,
    )
    large = start_copies(
        [(keys_hbm.at[0, i], keys_out.at[i]) for i in range(pieces)]
        + [(values_hbm.at[0, i], values_out.at[i]) for i in range(pieces)],
        piece_sems,
    )
    me = lax.axis_index("blk")
    z = lax.axis_index("req")
    chip, core = lax.shift_right_logical(me, 1), me & 1
    rows_ref[...] = jnp.zeros_like(rows_ref)
    for copy in small:
        copy.wait()
    count = near.shape[1]
    for n in range(count):
        for j in range(4):
            pair = near[j, n].astype(F32)
            for k in range(each):
                to = (j % 2) * POSITIONS + n
                rows_ref[j // 2, k, to : to + 1] = pair[k : k + 1]

    shape = (KEY_HEADS * ROWS, 2 * POSITIONS)
    column = lax.broadcasted_iota(jnp.int32, shape, 1)
    position = lax.broadcasted_iota(jnp.int32, shape, 0) % POSITIONS
    for k in range(each):
        live = ((column < POSITIONS) & (column < accepted_ref[0, k])) | (
            (column >= POSITIONS)
            & (column < POSITIONS + count)
            & (column - POSITIONS <= position)
        )
        query = unpack_rows(query_ref[k].astype(F32)).astype(BF16)
        got = attend(query, rows_ref[0, k].astype(BF16), rows_ref[1, k].astype(BF16), live, True)
        for j in range(3):
            own_out[j, k] = got[j]

    owners = owner_row[...]
    slot = lax.broadcasted_iota(jnp.int32, owners.shape, 1)
    for i in range(pieces):
        index = me * pieces + i
        owner = owner_ref[0, index]
        same = jnp.where((owners == owner) & (slot < index), 1.0, 0.0)
        rank = jnp.sum(same, axis=1, keepdims=True).astype(jnp.int32)
        place = place_of(owner, each, chip, core, kept)
        table_out[i : i + 1] = jnp.full((1, 128), place, jnp.int32)
        table_out[pieces + i : pieces + i + 1] = jnp.broadcast_to(
            length_ref[0, owner] - rank * rows, (1, 128)
        )
    for i in range(kept):
        request = ((chip ^ (i // each)) * 2 + core) * each + i % each
        group = group_ref[0, request]
        shift = z ^ lax.div(group, held)
        array = jnp.where(shift < 2, shift, (shift & ~1) + ((shift ^ core ^ 1) & 1))
        to = 2 * pieces + i
        table_out[to : to + 1] = jnp.full((1, 128), array * held + lax.rem(group, held), jnp.int32)
    for copy in large:
        copy.wait()


def pieces_kernel(chips, each, *refs):
    table_ref = refs[0]
    query_refs = refs[1 : 1 + chips]
    keys, values, mine_out = refs[1 + chips : 4 + chips]
    sibling_outs = refs[4 + chips : 6 + chips]
    queries_out, queries, acc = refs[6 + chips :]
    pieces, rows = keys.shape[0], keys.shape[1]
    kept = chips * each
    core = lax.axis_index("blk") & 1
    for j in range(chips):
        distance = jnp.where(core == 0, j, across_cores(j, chips))
        handed = j > 0 and j < chips - 1 and j % 2 == 0
        for side in range(2):
            start = (1 - side if handed else side) * each
            for k in range(each):
                query = unpack_rows(query_refs[j][start + k].astype(F32))
                queries[side * kept + distance * each + k] = query.astype(BF16)
    queries_out[...] = queries[:kept]
    lane = lax.broadcasted_iota(jnp.int32, (1, rows), 1)
    places = [jnp.max(table_ref[i : i + 1]) for i in range(pieces)]
    got = []
    for i in range(pieces):
        filled = table_ref[pieces + i : pieces + i + 1]
        live = lane < jnp.concatenate([filled] * (rows // 128), axis=1)
        got.append(attend(queries[places[i]], keys[i], values[i], live, True))
    acc[0] = jnp.full_like(acc[0], LOWEST)
    acc[1] = jnp.zeros_like(acc[1])
    acc[2] = jnp.zeros_like(acc[2])
    for i in range(pieces):
        acc[0, places[i]] = jnp.maximum(acc[0, places[i]], got[i][0])
    for i in range(pieces):
        lift = jnp.exp(got[i][0] - acc[0, places[i]])
        acc[1, places[i]] += lift * got[i][1]
        acc[2, places[i]] += lift * got[i][2]
    mine_out[...] = acc[:, :kept]
    for i in range(kept):
        half, at = divmod(i, kept // 2)
        sibling_outs[half][at] = pack_message(*[acc[j, kept + i] for j in range(3)])


def join_kernel(mine_ref, own_ref, first_ref, second_ref, out_ref):
    half, each = first_ref.shape[0], own_ref.shape[1]
    opened = open_messages([first_ref[i] for i in range(half)] + [second_ref[i] for i in range(half)])
    for i in range(2 * half):
        blocks = [[mine_ref[j, i] for j in range(3)], opened[i]]
        if i < each:
            blocks.append([own_ref[j, i] for j in range(3)])
        joined = merge(*blocks)
        for j in range(3):
            out_ref[j, i] = joined[j]


def prompts_kernel(chips, each, first_row, *refs):
    table_ref, query_ref, joined_ref = refs[:3]
    own_ref, sibling_ref, fetched_ref, swapped_ref = refs[3:7]
    out_refs = refs[7:]
    held, rows = own_ref.shape[0], own_ref.shape[1] // 2
    far = fetched_ref.shape[0] - 1
    pairs = [
        (lambda i: own_ref[i], lambda i: sibling_ref[i]),
        (lambda i: fetched_ref[far, i], lambda i: swapped_ref[far, i]),
    ]
    for p in range(0, far, 2):
        for ref in (fetched_ref, swapped_ref):
            pairs.append(tuple(lambda i, ref=ref, at=p + side: ref[at, i] for side in range(2)))
    lane = lax.broadcasted_iota(jnp.int32, (1, 2 * rows), 1)
    got = []
    for i in range(chips * each):
        at = jnp.max(table_ref[first_row + i : first_row + i + 1])
        array, slot = lax.div(at, held), lax.rem(at, held)

        def block(side):
            out = pairs[0][side](slot)
            for j in range(1, len(pairs)):
                out = jnp.where(array == j, pairs[j][side](slot), out)
            return out

        mine, other = block(0), block(1)
        marks = jnp.where(lane < rows, mine[:1, :1].astype(F32), other[:1, :1].astype(F32))
        got.append(
            attend(
                query_ref[i],
                jnp.concatenate([mine[:rows], other[:rows]], axis=0),
                jnp.concatenate([mine[rows:], other[rows:]], axis=0),
                marks < 0.5 * DEAD_MARK,
                False,
            )
        )
    for i in range(chips * each):
        merged = merge([joined_ref[j, i] for j in range(3)], got[i])
        out_refs[i // each][i % each] = pack_message(*merged)


def combine_kernel(chips, *refs):
    message_refs, out_ref = refs[:chips], refs[chips]
    count, each = out_ref.shape[1], out_ref.shape[2]
    low = lax.broadcasted_iota(jnp.int32, (POSITIONS, 128), 1) < HEAD_SIZE
    rows = []
    opened = open_messages([ref[k] for k in range(each) for ref in message_refs])
    for k in range(each):
        _, mass, part = merge(*opened[k * chips : (k + 1) * chips])
        out = part / mass
        swapped = swap_halves(out)
        columns = []
        for head in range(0, QUERY_HEADS, 2):
            c, g = head // GROUP, head % GROUP
            tile = slice((c // 2) * 128, (c // 2) * 128 + 128)
            first, second = (out, swapped) if c % 2 == 0 else (swapped, out)
            columns.append(
                jnp.where(
                    low,
                    first[g * POSITIONS : (g + 1) * POSITIONS, tile],
                    second[(g + 1) * POSITIONS : (g + 2) * POSITIONS, tile],
                )
            )
        rows.append(jnp.concatenate(columns, axis=1))
    for n in range(count):
        out_ref[0, n] = jnp.concatenate([row[n : n + 1] for row in rows], axis=0).astype(BF16)


HBM = pl.BlockSpec(memory_space=pltpu.HBM)
VMEM = pl.BlockSpec(memory_space=pltpu.VMEM)


def in_hbm(x):
    return pltpu.with_memory_space_constraint(x, pltpu.HBM)


def call(kernel, name, out_shape, in_specs, scratch=(), cost=0):
    many = isinstance(out_shape, (list, tuple))
    return pl.pallas_call(
        kernel,
        name=name,
        out_shape=out_shape,
        in_specs=in_specs,
        out_specs=[VMEM] * len(out_shape) if many else VMEM,
        scratch_shapes=list(scratch),
        cost_estimate=pl.CostEstimate(flops=0, bytes_accessed=cost, transcendentals=0),
        compiler_params=pltpu.CompilerParams(vmem_limit_bytes=VMEM_LIMIT),
    )


def per_device(
    devices,
    shifts,
    verified_queries,
    new_keys,
    verified_value_rows,
    prior_round_keys,
    prior_round_values,
    accepted,
    group_id,
    cache_len,
    slot_owner,
    piece_cache_keys,
    piece_cache_values,
    shared_prompt_keys,
    shared_prompt_values,
    prompt_mask,
):
    shape = jax.ShapeDtypeStruct
    each = verified_queries.shape[1]
    chips = devices // 2
    pieces, piece_rows = piece_cache_keys.shape[1:3]
    held, block_rows = shared_prompt_keys.shape[:2]
    kept = chips * each

    def other_core(x):
        return lax.ppermute(x, "blk", [(i, i ^ 1) for i in range(devices)])

    def other_chip(x, s):
        return lax.ppermute(x, "blk", [(i, i ^ (2 * s)) for i in range(devices)])

    def along_req(x, even, odd):
        pairs = []
        for i in range(devices * shifts):
            d, z = divmod(i, shifts)
            pairs.append((i, d * shifts + (z ^ (odd if d % 2 else even))))
        return lax.ppermute(x, ("blk", "req"), pairs)

    verified_queries, prior_round_keys, new_keys, prior_round_values, verified_value_rows = (
        jnp.transpose(x, (0, 2, 1, 3))
        for x in (
            verified_queries, prior_round_keys, new_keys, prior_round_values, verified_value_rows,
        )
    )
    near = (prior_round_keys, new_keys, prior_round_values, verified_value_rows)
    count = verified_queries.shape[1]
    block_size = 2 * block_rows
    piece_shape = (pieces, piece_rows, WIDTH)
    own_blocks, own_queries = call(
        parcel_kernel,
        "parcel",
        [
            shape((held, block_size, WIDTH), BF16),
            shape((each, MESSAGE, WIDTH), BF16),
        ],
        [HBM] * 4,
        [
            pltpu.SMEM((1, held), jnp.int32),
            pltpu.VMEM(verified_queries.shape, BF16),
            pltpu.VMEM((each, POSITIONS, QUERY_HEADS * HEAD_SIZE), F32),
            pltpu.SemaphoreType.DMA((4,)),
        ],
    )(
        *(
            in_hbm(x)
            for x in (prompt_mask.T, shared_prompt_keys, shared_prompt_values, verified_queries)
        )
    )
    sibling_blocks, sibling_queries, later_blocks = lax.optimization_barrier(
        (other_core(own_blocks), other_core(own_queries), own_blocks)
    )
    fetched = []
    for s in range(2, shifts, 2):
        fetched += [along_req(x, s + 1, s) for x in (own_blocks, sibling_blocks)]
    fetched.append(along_req(own_blocks, 1, 1))
    chip_queries = call(
        pair_kernel, "pair", shape((2 * each, MESSAGE, WIDTH), BF16), [VMEM] * 2
    )(own_queries, sibling_queries)

    own, table, keys, values = call(
        functools.partial(own_kernel, chips, each, shifts, held),
        "own",
        [
            shape((3, each, ROWS, WIDTH), F32),
            shape((2 * pieces + kept, 128), jnp.int32),
            shape(piece_shape, BF16),
            shape(piece_shape, BF16),
        ],
        [HBM] * 10 + [VMEM],
        [
            pltpu.SMEM(slot_owner.shape, jnp.int32),
            pltpu.SMEM(cache_len.shape, jnp.int32),
            pltpu.SMEM(accepted.shape, jnp.int32),
            pltpu.SMEM(group_id.shape, jnp.int32),
            pltpu.VMEM(slot_owner.shape, jnp.int32),
            pltpu.VMEM((4, count, each, WIDTH), BF16),
            pltpu.VMEM((2, each, 2 * POSITIONS, WIDTH), F32),
            pltpu.SemaphoreType.DMA((9,)),
            pltpu.SemaphoreType.DMA((2 * pieces,)),
        ],
        8 * 1024 * 1024,
    )(
        *(
            in_hbm(x)
            for x in (slot_owner, cache_len, accepted, group_id)
            + near
            + (piece_cache_keys, piece_cache_values)
        ),
        chip_queries,
    )

    queries = [chip_queries]
    for s in range(1, chips - 1, 2):
        taken = lax.ppermute(
            chip_queries,
            "blk",
            [(i, i ^ (2 * (across_cores(s, chips) if i % 2 else s))) for i in range(devices)],
        )
        taken = lax.optimization_barrier((taken, table))[0]
        queries += [taken, other_core(taken)]
    if chips > 1:
        queries.append(other_chip(chip_queries, chips - 1))

    wide = (kept, ROWS, WIDTH)
    mine, *to_sibling, kept_queries = call(
        functools.partial(pieces_kernel, chips, each),
        "pieces",
        [shape((3,) + wide, F32)]
        + [shape((kept // 2, MESSAGE, WIDTH), F32)] * 2
        + [shape(wide, BF16)],
        [VMEM] * (chips + 3),
        [
            pltpu.VMEM((2 * kept, ROWS, WIDTH), BF16),
            pltpu.VMEM((3, 2 * kept, ROWS, WIDTH), F32),
        ],
    )(table, *queries, keys, values)
    from_sibling = [other_core(x) for x in to_sibling]
    joined = call(join_kernel, "join", shape((3,) + wide, F32), [VMEM] * 4)(
        mine, own, *from_sibling
    )
    fetched = lax.optimization_barrier((kept_queries, *fetched))[1:]
    gathered = call(
        gather_kernel,
        "gather",
        shape((len(fetched), held, block_size, WIDTH), BF16),
        [VMEM] * len(fetched),
    )(*fetched)

    messages = call(
        functools.partial(prompts_kernel, chips, each, 2 * pieces),
        "prompts",
        [shape((each, MESSAGE, WIDTH), F32)] * chips,
        [VMEM] * 7,
    )(table, kept_queries, joined, own_blocks, sibling_blocks, gathered, other_core(gathered))
    arrived = [messages[0]] + [other_chip(messages[s], s) for s in range(chips - 1, 0, -1)]

    out = call(
        functools.partial(combine_kernel, chips),
        "combine",
        shape(verified_queries.shape, BF16),
        [VMEM] * chips,
    )(*arrived)
    return jnp.transpose(out, (0, 2, 1, 3))


def solution(mesh):
    placed = (
        P("req", "blk", None, None),
        P("req", "blk", None, None),
        P("req", "blk", None, None),
        P("req", "blk", None, None),
        P("req", "blk", None, None),
        P("req", "blk"),
        P("req", None),
        P("req", None),
        P("req", None),
        P("req", "blk", None, None),
        P("req", "blk", None, None),
        P("req", "blk", None),
        P("req", "blk", None),
        P("req", "blk"),
    )
    return jax.shard_map(
        functools.partial(per_device, mesh.shape["blk"], mesh.shape["req"]),
        mesh=mesh,
        in_specs=placed,
        out_specs=P("req", "blk", None, None),
        check_vma=False,
    )
```
